32 devices in a mesh: parts: 2 (over y), tensor: 16 (over z, x, core).
Axes of the slice: x: 2, y: 2, z: 4, core: 2. Of those that a mesh axis runs over, the one named last changes fastest.
Arguments:
- cotangent: bfloat16 [384, 8192], P(('parts', 'tensor')), parts along dimension 0, may hold values from -6 to 6
- hidden: bfloat16 [384, 28672], P('parts', 'tensor'), parts along dimension 0, may hold values from -6 to 6
- down_weight: bfloat16 [28672, 8192], P('tensor'), may hold values from -0.0625 to 0.0625
- adapter_in: bfloat16 [28672, 2560], P('tensor'), may hold values from -0.119628906 to 0.119628906
- adapter_out: bfloat16 [2560, 8192], P(None, 'tensor'), may hold values from -0.0625 to 0.0625
- segment_ids: int32 [384], P('parts'), parts along dimension 0, may hold values from 0 to 11, never falling along the last dimension, each value on 1 to 32 neighbouring positions
- segment_dirs: int32 [24], P('parts'), parts along dimension 0, may hold values from 0 to 39
Outputs:
- grad_hidden: bfloat16 [384, 28672], P('parts', 'tensor'), parts along dimension 0
- grad_in: float32 [57344, 2560], P(('parts', 'tensor')), parts along dimension 0
- grad_out: float32 [5120, 8192], P('parts', 'tensor'), parts along dimension 0
The draws below stay inside these ranges and needn't reach their ends.
There are 2 independent parts, one for each index of `parts`. The reference program is written for one: setup_inputs(seed, part) draws one part's arguments, and reference() takes and returns one part's arrays. A program takes and returns all parts, laid end to end along the dimension named above; an argument that names none is the same for every part. Nothing has to cross between parts.
Inputs may be any that keep to these rules, and one draw needn't show every extreme that they name: `segment_ids`: segment numbers never fall along the tokens; each segment holds 1 to 32 tokens.
All inputs are finite; a program needn't handle non-finite values.
Results may differ from the reference program's by a relative error of at most 0.005.
Values may be sent and summed in bfloat16 or wider, within the bound.
A program may use at most 192 MiB of HBM per device.

```python
import math
import jax
import jax.numpy as jnp
import numpy as np
from jax import lax

D = 8192
FF = 28672
RANK = 64
NUM_DIR = 40
MOST = 32
TOKENS = 192
NSEG = 12


def with_ends(entries, stream_key, least, high):
    longest = entries.shape.index(max(entries.shape))
    spots = []
    for shift in (0, 1):
        where = [jax.random.randint(jax.random.fold_in(stream_key, axis), (), 0, length) for axis, length in enumerate(entries.shape)]
        where[longest] = (where[longest] + shift) % entries.shape[longest]
        spots.append(tuple(where))
    return entries.at[spots[0]].set(least).at[spots[1]].set(high)


def block_levels(own_key, dims, pieces, least, high):
    def one(axis_at, blocks):
        steps = jax.random.uniform(jax.random.fold_in(jax.random.fold_in(own_key, 6), axis_at), (blocks,), jnp.float32, least / len(pieces), high / len(pieces))
        return jnp.repeat(jnp.exp(steps), dims[axis_at] // blocks).reshape((-1,) + (1,) * (len(dims) - axis_at - 1))

    factor_of = one(*pieces[0])
    for cut in pieces[1:]:
        factor_of = factor_of * one(*cut)
    return factor_of


def cumulative_ranks(number_of, slope):
    portions = [(1 << 20) // math.isqrt(rank ** slope) + 1 for rank in range(1, number_of + 1)]
    width = 1 + sum(portions) // (1 << 30)
    return np.cumsum(np.array([max(1, weight // width) for weight in portions]))


def skewed_ids(rng, shape, number_of, lean):
    grid = cumulative_ranks(number_of, lean)
    lot = jax.random.randint(jax.random.fold_in(rng, 1), shape, 0, int(grid[number_of - 1]))
    standing = jnp.searchsorted(jnp.asarray(grid, jnp.int32), lot, side="right")
    return jax.random.permutation(jax.random.fold_in(rng, 2), number_of)[standing].astype(jnp.int32)


def length_profile(number_of, total, limit, skew):
    portions = [(1 << 20) // math.isqrt(rank ** skew) + 1 for rank in range(2, number_of + 1)]
    surplus, counts = total - limit - (number_of - 1), [1] * (number_of - 1)
    while surplus > 0:
        candidates = [i for i in range(number_of - 1) if counts[i] < limit]
        pool, left = sum([portions[i] for i in candidates]), surplus
        for i in candidates:
            more = min(limit - counts[i], max(1, left * portions[i] // pool), surplus)
            counts[i] = counts[i] + more
            surplus = surplus - more
    return np.array([limit] + counts)


def uneven_parts(rng, amount, total, bound, slope):
    if amount == 2:
        one = jax.random.randint(rng, (), max(1, total - bound), min(bound, total - 1) + 1)
        return jnp.stack([one, total - one])
    sizes = jnp.asarray(length_profile(amount, total, bound, slope), jnp.int32)
    pairs = (amount - 1) // 2
    source_of, receiver = sizes[1:1 + 2 * pairs:2], sizes[2:2 + 2 * pairs:2]
    slack = jnp.minimum(source_of - 1, bound - receiver)
    shifted = jax.random.randint(jax.random.fold_in(rng, 1), (pairs,), 0, 1 << 20) % (slack + 1)
    sizes = sizes.at[1:1 + 2 * pairs:2].set(source_of - shifted).at[2:2 + 2 * pairs:2].set(receiver + shifted)
    return sizes[jax.random.permutation(jax.random.fold_in(rng, 2), amount)]


def gaussian(stream_key, shape, scale, most, shards=(), kind=jnp.bfloat16):
    entries = jax.random.normal(stream_key, shape, jnp.float32) * scale
    if len(shards) > 0:
        entries = block_levels(stream_key, shape, shards, -0.22, 0.18) * entries
    return jnp.clip(entries, min=-most, max=most).astype(kind)


def setup_inputs(seed: int = 0, part: int = 0) -> dict:
    key_of = jax.random.split(jax.random.key(seed), 8)
    part_keys = jax.random.split(jax.random.fold_in(key_of[7], part), 8)
    cotangent = gaussian(part_keys[0], (TOKENS, D), 1.0, 6.0, ((0, 16),))
    hidden = gaussian(part_keys[1], (TOKENS, FF), 1.0, 6.0, ((1, 16),))
    down_weight = gaussian(key_of[2], (FF, D), D ** -0.5, 0.0625, ((0, 16),))
    adapter_in = gaussian(key_of[3], (FF, NUM_DIR * RANK), 0.02, 0.119628906, ((0, 16),))
    adapter_out = gaussian(key_of[4], (NUM_DIR * RANK, D), D ** -0.5, 0.0625, ((1, 16),))
    segment_ids = jnp.searchsorted(jnp.cumsum(uneven_parts(part_keys[5], NSEG, TOKENS, MOST, 2)), jnp.arange(TOKENS), side="right").astype(jnp.int32)
    segment_dirs = with_ends(skewed_ids(part_keys[6], (NSEG,), NUM_DIR, 2), jax.random.fold_in(part_keys[6], 3), 0, NUM_DIR - 1).astype(jnp.int32)
    return {"cotangent": cotangent, "hidden": hidden, "down_weight": down_weight, "adapter_in": adapter_in, "adapter_out": adapter_out, "segment_ids": segment_ids, "segment_dirs": segment_dirs}


def reference(cotangent, hidden, down_weight, adapter_in, adapter_out, segment_ids, segment_dirs):
    seg_hot = (segment_ids[:, None] == jnp.arange(NSEG, dtype=jnp.int32)[None, :]).astype(jnp.float32)
    dir_hot = (segment_dirs[:, None] == jnp.arange(NUM_DIR, dtype=jnp.int32)[None, :]).astype(jnp.float32)
    onehot = jnp.dot(seg_hot, dir_hot, precision=lax.Precision.HIGHEST)
    wide_u = lax.dot_general(cotangent, adapter_out, (((1,), (1,)), ((), ())), preferred_element_type=jnp.float32)
    wide_v = jnp.dot(hidden, adapter_in, preferred_element_type=jnp.float32)
    low_u = jnp.sum(wide_u.reshape(TOKENS, NUM_DIR, RANK) * onehot[:, :, None], axis=1)
    low_v = jnp.sum(wide_v.reshape(TOKENS, NUM_DIR, RANK) * onehot[:, :, None], axis=1)
    spread_u = (0.5 * onehot[:, :, None] * low_u[:, None, :]).reshape(TOKENS, NUM_DIR * RANK).astype(jnp.bfloat16)
    spread_v = (0.5 * onehot[:, :, None] * low_v[:, None, :]).reshape(TOKENS, NUM_DIR * RANK).astype(jnp.bfloat16)
    base = lax.dot_general(cotangent, down_weight, (((1,), (1,)), ((), ())), preferred_element_type=jnp.float32)
    extra = lax.dot_general(spread_u, adapter_in, (((1,), (1,)), ((), ())), preferred_element_type=jnp.float32)
    grad_hidden = (base + extra).astype(jnp.bfloat16)
    grad_in = lax.dot_general(hidden, spread_u, (((0,), (0,)), ((), ())), preferred_element_type=jnp.float32)
    grad_out = lax.dot_general(spread_v, cotangent, (((0,), (0,)), ((), ())), preferred_element_type=jnp.float32)
    return (grad_hidden, grad_in, grad_out)
```

```python
import functools

import jax
import jax.numpy as jnp
from jax import lax
from jax.experimental import pallas as pl
from jax.experimental.pallas import tpu as pltpu
from jax.sharding import PartitionSpec as P

RANK = 64
NUM_DIR = 40
WIDE = RANK * NUM_DIR
MESH = pl.DeviceIdType.MESH
F32 = jnp.float32
BF16 = jnp.bfloat16
NT = (((1,), (1,)), ((), ()))
TN = (((0,), (0,)), ((), ()))
NN = (((1,), (0,)), ((), ()))
PAD = 16
CHUNKS = 4


def dot(lhs, rhs, dims, **kw):
    return lax.dot_general(lhs, rhs, dims, preferred_element_type=F32, **kw)


def iota(shape, axis):
    return lax.broadcasted_iota(jnp.int32, shape, axis)


def direction_table(segment_ids, segment_dirs):
    seg_hot = (
        segment_ids[:, None] == jnp.arange(segment_dirs.shape[0], dtype=jnp.int32)[None, :]
    ).astype(F32)
    dir_hot = (segment_dirs[:, None] == jnp.arange(NUM_DIR, dtype=jnp.int32)[None, :]).astype(F32)
    return jnp.dot(seg_hot, dir_hot, precision=lax.Precision.HIGHEST)


def select_rank(wide, onehot):
    count = wide.shape[0]
    return jnp.sum(wide.reshape(count, NUM_DIR, RANK) * onehot[:, :, None], axis=1)


def spread_rank(low, onehot):
    count = low.shape[0]
    return (
        (0.5 * onehot[:, :, None] * low[:, None, :]).reshape(count, NUM_DIR * RANK).astype(BF16)
    )


def per_device_plain(
    cotangent, hidden, down_weight, adapter_in, adapter_out, segment_ids, segment_dirs
):
    onehot = direction_table(segment_ids, segment_dirs)
    width_share = adapter_out.shape[1]
    shards = cotangent.shape[1] // width_share
    own = cotangent.shape[0]
    full_rows = lax.all_gather(cotangent, "tensor", axis=0, tiled=True)
    pieces = cotangent.reshape(own, shards, width_share).transpose(1, 0, 2)
    columns = lax.all_to_all(pieces, "tensor", 0, 0, tiled=True).reshape(shards * own, width_share)
    wide_u = dot(columns, adapter_out, NT)
    wide_v = dot(hidden, adapter_in, NN)
    part = jnp.concatenate([select_rank(wide_u, onehot), select_rank(wide_v, onehot)], axis=1)
    low = lax.psum(part, "tensor")
    spread_u = spread_rank(low[:, :RANK], onehot)
    spread_v = spread_rank(low[:, RANK:], onehot)
    grad_in = dot(hidden, spread_u, TN)
    grad_out = dot(spread_v, columns, TN)
    base = dot(full_rows, down_weight, NT)
    extra = dot(spread_u, adapter_in, NT)
    return ((base + extra).astype(BF16), grad_in, grad_out)


def direction_columns(place, dir_row):
    ones = jnp.ones((place.shape[1], 128), BF16)
    found = dot((place * (dir_row + 1.0)).astype(BF16), ones, NN)
    return found - 1.0


def padded_place(own, tokens, rows, flip):
    shape = (tokens, rows) if flip else (rows, tokens)
    row, token = (iota(shape, 1), iota(shape, 0)) if flip else (iota(shape, 0), iota(shape, 1))
    inside = lax.rem(row, PAD)
    return ((token == own * (row // PAD) + inside) & (inside < own)).astype(F32)


def half_shift(shape):
    return (iota(shape, 1) >= RANK).astype(F32)


def main_kernel(
    cot_hbm, hid_hbm, dw_hbm, ain_hbm, aout_hbm, ids_ref, dirs_ref,
    gh_ref, low_ref, cols_ref,
    cot, cot16, gat, fourth, dw, ain, aout, hid, acc, wide_cols, lpart, rpart, low, spread, perm,
    ld_sem, gs_sem, gr_sem, sib_sem, x_sem, cs_sem, chain_sem,
):
    own, width = cot_hbm.shape
    tokens, ff = hid_hbm.shape
    share = aout_hbm.shape[1]
    shards = width // share
    rows = shards * PAD
    quarter = width // 4
    step = quarter // CHUNKS

    p = lax.axis_index("parts")
    me = lax.axis_index("tensor")
    z, x, c = me // 4, lax.rem(me // 2, 2), lax.rem(me, 2)
    zs = [z, z + 1 - 2 * lax.rem(z, 2), lax.rem(z + 2, 4), 3 - z]
    inner = (z == 1) | (z == 2)

    def index(zz, xx, cc):
        return zz * 4 + xx * 2 + cc

    sib = index(z, x, 1 - c)
    xnb = index(z, 1 - x, c)
    z1, z2, z3 = (index(zs[k], x, c) for k in (1, 2, 3))

    def dev(i):
        return (p, i)

    bar = pltpu.get_barrier_semaphore()
    for nb in (sib, xnb, z1, z2):
        pl.semaphore_signal(bar, inc=1, device_id=dev(nb), device_id_type=MESH)

    @pl.when(inner)
    def _():
        pl.semaphore_signal(bar, inc=1, device_id=dev(z3), device_id_type=MESH)

    ld_cot = pltpu.make_async_copy(cot_hbm, cot, ld_sem.at[0])
    ld_hid = pltpu.make_async_copy(hid_hbm, hid, ld_sem.at[1])
    ld_cot.start()
    ld_hid.start()
    n_ain = WIDE // 512
    ld_ain = []
    for i in range(n_ain):
        cut = pl.ds(512 * i, 512)
        ld_ain.append(
            pltpu.make_async_copy(ain_hbm.at[:, cut], ain.at[:, cut], ld_sem.at[2 + i])
        )
        ld_ain[-1].start()
    ld_aout = pltpu.make_async_copy(aout_hbm, aout, ld_sem.at[2 + n_ain])
    ld_aout.start()
    for q in range(CHUNKS):
        for j in range(4):
            cut = pl.ds(quarter * j + step * q, step)
            pltpu.make_async_copy(
                dw_hbm.at[:, cut], dw.at[:, cut], ld_sem.at[3 + n_ain + q]
            ).start()

    def wait_dw(q):
        cut = pl.ds(quarter * q, quarter)
        pltpu.make_async_copy(dw_hbm.at[:, cut], dw.at[:, cut], ld_sem.at[3 + n_ain + q]).wait()

    def rows_of(b):
        return pl.ds(pl.multiple_of(b * PAD, PAD), PAD)

    def piece(b, q):
        return gat.at[:, rows_of(b), pl.ds(step * q, step)]

    def send(b, q, to, sem, recv):
        pltpu.make_async_remote_copy(
            src_ref=piece(b, q), dst_ref=piece(b, q), send_sem=sem, recv_sem=recv,
            device_id=dev(to), device_id_type=MESH,
        ).start()

    def arrived(b, q, sem):
        pltpu.make_async_copy(piece(b, q), piece(b, q), sem).wait()

    def col_block(k):
        return index(zs[k], x, c)

    def x_block(k):
        return index(zs[k], 1 - x, c)

    def send_own(q):
        send(me, q, xnb, gs_sem.at[0], x_sem.at[q])
        send(me, q, z1, gs_sem.at[0], gr_sem.at[q])
        send(me, q, z2, gs_sem.at[0], gr_sem.at[CHUNKS + q])

        @pl.when(inner)
        def _():
            send(me, q, z3, gs_sem.at[1], gr_sem.at[2 * CHUNKS + q])

        send(me, q, sib, gs_sem.at[0], sib_sem.at[q])

    def take_column(k, q):
        b = col_block(k)
        arrived(b, q, gr_sem.at[(k - 1) * CHUNKS + q])
        send(b, q, xnb, gs_sem.at[0], x_sem.at[k * CHUNKS + q])
        if k == 2:

            @pl.when(inner)
            def _():
                send(b, q, z1, gs_sem.at[1], gr_sem.at[2 * CHUNKS + q])

        send(b, q, sib, gs_sem.at[0], sib_sem.at[q])

    def take_x(k, q):
        b = x_block(k)
        arrived(b, q, x_sem.at[k * CHUNKS + q])
        send(b, q, sib, gs_sem.at[0], sib_sem.at[q])

    def take_sib(q):
        half = gat.at[:, pl.ds(0, rows // 2), pl.ds(step * q, step)]
        pltpu.make_async_copy(half, half, sib_sem.at[q]).wait()

    chain = (z1, z2, xnb, sib)

    def greet(i):
        pl.semaphore_signal(chain_sem.at[i], inc=1, device_id=dev(chain[i]), device_id_type=MESH)

    def greeted(i):
        pl.semaphore_wait(chain_sem.at[i], 1)

    ld_cot.wait()
    cot32 = cot[...].astype(F32)
    zero4 = jnp.zeros((PAD - own, width), F32)
    cot16[...] = jnp.concatenate([cot32, zero4], axis=0).astype(BF16)
    gap = PAD - own
    for j in range(3):
        tile = jnp.concatenate(
            [
                cot32[:, quarter * j : quarter * (j + 1)],
                cot32[gap * j : gap * (j + 1), 3 * quarter :],
            ],
            axis=0,
        )
        gat[j, rows_of(me), :] = tile.astype(BF16)
    pl.semaphore_wait(bar, 4 + z * (3 - z) // 2)
    send_own(0)
    send_own(1)
    greet(0)

    dir_row = jnp.zeros((1, tokens), F32)
    ids = ids_ref[...]
    for s in range(dirs_ref.shape[0]):
        dir_row = jnp.where(ids == s, dirs_ref[s].astype(F32), dir_row)
    pad_place = padded_place(own, tokens, rows, False)
    dense_place = (iota((tokens, tokens), 0) == iota((tokens, tokens), 1)).astype(F32)
    dirs_dense = direction_columns(dense_place, dir_row) - half_shift((tokens, 128))
    dirs_pad = direction_columns(pad_place, dir_row) - half_shift((rows, 128))
    for j in range(3):
        a, b = iota((rows, rows), 0), iota((rows, rows), 1)
        ra, rb = lax.rem(a, PAD), lax.rem(b, PAD)
        hit = (a // PAD == b // PAD) & (ra // gap == j) & (rb - own == ra - gap * j)
        perm[j] = hit.astype(BF16)

    def pick(total, wide, where, first):
        for i in range(wide.shape[1] // 128):
            total = total + jnp.where(
                where == float(first + 2 * i), wide[:, 128 * i : 128 * (i + 1)], 0.0
            )
        return total

    ld_hid.wait()
    tot_v = jnp.zeros((tokens, 128), F32)
    for i in range(n_ain):
        ld_ain[i].wait()
        wide = dot(hid[...], ain[:, 512 * i : 512 * (i + 1)], NN)
        tot_v = pick(tot_v, wide, dirs_dense, 8 * i)
        if i == 1:
            greeted(0)
            greet(1)
    tot_v = dot(pad_place, tot_v, NN, precision=lax.Precision.HIGHEST)
    v = tot_v + pltpu.roll(tot_v, RANK, 1)

    take_column(1, 0)
    greeted(1)
    greet(2)
    take_x(0, 0)
    take_column(2, 0)
    send_own(2)
    greeted(2)
    greet(3)
    take_column(3, 0)
    take_x(1, 0)
    greeted(3)

    def cols_of(d):
        return pl.ds(pl.multiple_of(d * share, share), share)

    for i in range(1, shards):
        d = lax.rem(me + i, shards)
        pltpu.make_async_remote_copy(
            src_ref=cot16.at[:, cols_of(d)], dst_ref=wide_cols.at[rows_of(me), :],
            send_sem=cs_sem.at[0], recv_sem=cs_sem.at[1],
            device_id=dev(d), device_id_type=MESH,
        ).start()
    wide_cols[rows_of(me), :] = cot16[:, cols_of(me)]
    send_own(3)
    take_column(1, 1)
    take_x(2, 0)
    take_x(0, 1)
    take_column(2, 1)
    take_x(3, 0)
    others = wide_cols.at[pl.ds(0, rows - PAD), :]
    pltpu.make_async_copy(others, others, cs_sem.at[1]).wait()
    ld_aout.wait()
    tot_u = jnp.zeros((rows, 128), F32)
    for i in range(n_ain):
        wide = dot(wide_cols[...], aout[512 * i : 512 * (i + 1), :], NT)
        tot_u = pick(tot_u, wide, dirs_pad, 8 * i)
    u = tot_u + pltpu.roll(tot_u, RANK, 1)
    lpart[...] = jnp.where(iota((rows, 128), 1) < RANK, u, v)
    for i in range(1, shards):
        d = lax.rem(me + i, shards)
        pltpu.make_async_remote_copy(
            src_ref=lpart.at[rows_of(d), :], dst_ref=rpart.at[me],
            send_sem=cs_sem.at[2], recv_sem=cs_sem.at[3],
            device_id=dev(d), device_id_type=MESH,
        ).start()
    rpart[me] = lpart[rows_of(me), :]

    take_column(1, 2)
    take_column(3, 1)
    take_x(1, 1)
    take_x(2, 1)

    def assemble(q):
        cut = pl.ds(step * q, step)
        total = dot(perm[0], gat[0, :, cut], NN)
        total += dot(perm[1], gat[1, :, cut], NN)
        total += dot(perm[2], gat[2, :, cut], NN)
        fourth[...] = total.astype(BF16)

    tile = ff // 2

    def base(q, h):
        r = pl.ds(tile * h, tile)
        total = acc[r, :] if q > 0 else None
        for j in range(4):
            cut = slice(quarter * j + step * q, quarter * j + step * (q + 1))
            rhs = fourth[...] if j == 3 else gat[j, :, step * q : step * (q + 1)]
            add = dot(dw[r, cut], rhs, NT)
            total = add if total is None else total + add
        acc[r, :] = total

    take_sib(0)
    wait_dw(0)
    assemble(0)
    base(0, 0)
    pltpu.make_async_copy(rpart.at[pl.ds(0, shards - 1)], rpart.at[pl.ds(0, shards - 1)], cs_sem.at[3]).wait()
    summed = rpart[0]
    for i in range(1, shards):
        summed = summed + rpart[i]
    low[rows_of(me), :] = (0.5 * summed).astype(BF16)
    for i in range(1, shards):
        d = lax.rem(me + i, shards)
        pltpu.make_async_remote_copy(
            src_ref=low.at[rows_of(me), :], dst_ref=low.at[rows_of(me), :],
            send_sem=cs_sem.at[4], recv_sem=cs_sem.at[5],
            device_id=dev(d), device_id_type=MESH,
        ).start()
    take_x(0, 2)
    take_column(2, 2)
    take_x(3, 1)
    take_column(1, 3)
    take_x(0, 3)
    base(0, 1)
    take_column(3, 2)
    take_x(1, 2)
    take_column(2, 3)
    take_x(2, 2)
    take_sib(1)
    wait_dw(1)
    assemble(1)
    base(1, 0)
    take_column(3, 3)
    take_x(3, 2)
    take_x(1, 3)
    base(1, 1)
    take_x(2, 3)
    take_x(3, 3)
    take_sib(2)
    wait_dw(2)
    assemble(2)
    base(2, 0)
    base(2, 1)
    known = low.at[pl.ds(0, rows - PAD), :]
    pltpu.make_async_copy(known, known, cs_sem.at[5]).wait()
    both = low[...].astype(F32)
    u_twice = jnp.where(iota((rows, 128), 1) < RANK, both, pltpu.roll(both, RANK, 1))
    for i in range(NUM_DIR // 2):
        spread[:, 128 * i : 128 * (i + 1)] = jnp.where(
            dirs_pad == float(2 * i), u_twice, 0.0
        ).astype(BF16)
    take_sib(3)
    wait_dw(3)
    assemble(3)
    base(3, 0)
    base(3, 1)
    place = padded_place(own, tokens, rows, True).astype(BF16)
    for h in range(2):
        r = pl.ds(tile * h, tile)
        total = acc[r, :] + dot(ain[r, :], spread[...], NT)
        gh_ref[:, r] = dot(place, total.astype(BF16), NT).astype(BF16)
    low_ref[...] = low[...]
    cols_ref[...] = wide_cols[...]

    most = gat.at[:, pl.ds(0, 14 * PAD), :]
    pltpu.make_async_copy(most, most, gs_sem.at[0]).wait()

    @pl.when(inner)
    def _():
        few = gat.at[:, pl.ds(0, 2 * PAD), :]
        pltpu.make_async_copy(few, few, gs_sem.at[1]).wait()

    pltpu.make_async_copy(others, others, cs_sem.at[0]).wait()
    pltpu.make_async_copy(rpart.at[pl.ds(0, shards - 1)], rpart.at[pl.ds(0, shards - 1)], cs_sem.at[2]).wait()
    pltpu.make_async_copy(known, known, cs_sem.at[4]).wait()


def write_kernel(
    gh_ref, low_ref, cols_ref, hid_ref, ids_ref, dirs_ref, own,
    gh_hbm, gin_hbm, gout_hbm, gin, gout, spread, spread_v, sem,
):
    tokens, ff = hid_ref.shape
    rows = low_ref.shape[0]
    put_gh = pltpu.make_async_copy(gh_ref, gh_hbm, sem.at[0])
    put_gh.start()
    dir_row = jnp.zeros((1, tokens), F32)
    ids = ids_ref[...]
    for s in range(dirs_ref.shape[0]):
        dir_row = jnp.where(ids == s, dirs_ref[s].astype(F32), dir_row)
    pad_place = padded_place(own, tokens, rows, False)
    dense_place = (iota((tokens, tokens), 0) == iota((tokens, tokens), 1)).astype(F32)
    dirs_dense = direction_columns(dense_place, dir_row) - half_shift((tokens, 128))
    dirs_pad = direction_columns(pad_place, dir_row) - half_shift((rows, 128))
    place = padded_place(own, tokens, rows, True).astype(BF16)
    dense = dot(place, low_ref[...], NN)
    u_twice = jnp.where(iota((tokens, 128), 1) < RANK, dense, pltpu.roll(dense, RANK, 1))
    for i in range(NUM_DIR // 2):
        spread[:, 128 * i : 128 * (i + 1)] = jnp.where(
            dirs_dense == float(2 * i), u_twice, 0.0
        ).astype(BF16)
    puts = [put_gh]
    tile = 256
    for i in range(ff // tile):
        r = pl.ds(tile * i, tile)
        gin[r, :] = dot(hid_ref[:, tile * i : tile * (i + 1)], spread[...], TN)
        puts.append(pltpu.make_async_copy(gin.at[r, :], gin_hbm.at[r, :], sem.at[1 + i]))
        puts[-1].start()
    base = 1 + ff // tile
    both = low_ref[...].astype(F32)
    v_twice = jnp.where(iota((rows, 128), 1) < RANK, pltpu.roll(both, RANK, 1), both)
    for i in range(NUM_DIR // 2):
        spread_v[:, 128 * i : 128 * (i + 1)] = jnp.where(
            dirs_pad == float(2 * i), v_twice, 0.0
        ).astype(BF16)
    for i in range(WIDE // 512):
        r = pl.ds(512 * i, 512)
        gout[r, :] = dot(spread_v[:, 512 * i : 512 * (i + 1)], cols_ref[...], TN)
        puts.append(pltpu.make_async_copy(gout.at[r, :], gout_hbm.at[r, :], sem.at[base + i]))
        puts[-1].start()
    for put in puts:
        put.wait()


def per_device(cotangent, hidden, down_weight, adapter_in, adapter_out, segment_ids, segment_dirs):
    own, width = cotangent.shape
    tokens, ff = hidden.shape
    share = adapter_out.shape[1]
    shards = width // share
    rows = shards * PAD
    ids = segment_ids.reshape(1, tokens)
    any_space = pl.BlockSpec(memory_space=pl.ANY)
    vmem = pl.BlockSpec(memory_space=pltpu.VMEM)
    smem = pl.BlockSpec(memory_space=pltpu.SMEM)
    n_loads = 3 + WIDE // 512 + CHUNKS
    gh, low, cols = pl.pallas_call(
        main_kernel,
        out_shape=(
            jax.ShapeDtypeStruct((tokens, ff), BF16),
            jax.ShapeDtypeStruct((rows, 128), BF16),
            jax.ShapeDtypeStruct((rows, share), BF16),
        ),
        in_specs=[any_space] * 5 + [vmem, smem],
        out_specs=(vmem, vmem, vmem),
        scratch_shapes=[
            pltpu.VMEM((own, width), BF16),
            pltpu.VMEM((PAD, width), BF16),
            pltpu.VMEM((3, rows, width // 4), BF16),
            pltpu.VMEM((rows, width // 4 // CHUNKS), BF16),
            pltpu.VMEM((ff, width), BF16),
            pltpu.VMEM((ff, WIDE), BF16),
            pltpu.VMEM((WIDE, share), BF16),
            pltpu.VMEM((tokens, ff), BF16),
            pltpu.VMEM((ff, rows), F32),
            pltpu.VMEM((rows, share), BF16),
            pltpu.VMEM((rows, 128), F32),
            pltpu.VMEM((shards, PAD, 128), F32),
            pltpu.VMEM((rows, 128), BF16),
            pltpu.VMEM((rows, WIDE), BF16),
            pltpu.VMEM((3, rows, rows), BF16),
            pltpu.SemaphoreType.DMA((n_loads,)),
            pltpu.SemaphoreType.DMA((2,)),
            pltpu.SemaphoreType.DMA((3 * CHUNKS,)),
            pltpu.SemaphoreType.DMA((CHUNKS,)),
            pltpu.SemaphoreType.DMA((4 * CHUNKS,)),
            pltpu.SemaphoreType.DMA((6,)),
            pltpu.SemaphoreType.REGULAR((4,)),
        ],
        compiler_params=pltpu.CompilerParams(
            collective_id=0, has_side_effects=True, vmem_limit_bytes=56 << 20
        ),
        cost_estimate=pl.CostEstimate(
            flops=2 * rows * ff * width, bytes_accessed=2 * ff * (width + WIDE), transcendentals=0
        ),
    )(cotangent, hidden, down_weight, adapter_in, adapter_out, ids, segment_dirs)
    writer = functools.partial(_write, own)
    return pl.pallas_call(
        writer,
        out_shape=(
            jax.ShapeDtypeStruct((tokens, ff), BF16),
            jax.ShapeDtypeStruct((ff, WIDE), F32),
            jax.ShapeDtypeStruct((WIDE, share), F32),
        ),
        in_specs=[vmem] * 5 + [smem],
        out_specs=(any_space,) * 3,
        scratch_shapes=[
            pltpu.VMEM((ff, WIDE), F32),
            pltpu.VMEM((WIDE, share), F32),
            pltpu.VMEM((tokens, WIDE), BF16),
            pltpu.VMEM((rows, WIDE), BF16),
            pltpu.SemaphoreType.DMA((1 + ff // 256 + WIDE // 512,)),
        ],
        compiler_params=pltpu.CompilerParams(vmem_limit_bytes=48 << 20),
        cost_estimate=pl.CostEstimate(
            flops=2 * tokens * ff * WIDE, bytes_accessed=4 * WIDE * (ff + share), transcendentals=0
        ),
    )(gh, low, cols, hidden, ids, segment_dirs)


def _write(own, gh, low, cols, hid, ids, dirs, *rest):
    write_kernel(gh, low, cols, hid, ids, dirs, own, *rest)


def solution(mesh):
    def body(cotangent, hidden, *rest):
        own, width = cotangent.shape
        ff = hidden.shape[1]
        share = width // mesh.shape["tensor"]
        fits = (
            mesh.shape["tensor"] == 16
            and own == 12
            and hidden.shape[0] == 16 * own
            and width % (4 * CHUNKS * 128) == 0
            and share % 128 == 0
            and ff % 256 == 0
        )
        return (per_device if fits else per_device_plain)(cotangent, hidden, *rest)

    return jax.shard_map(
        body,
        mesh=mesh,
        in_specs=(
            P(("parts", "tensor"), None),
            P("parts", "tensor"),
            P("tensor", None),
            P("tensor", None),
            P(None, "tensor"),
            P("parts"),
            P("parts"),
        ),
        out_specs=(P("parts", "tensor"), P(("parts", "tensor"), None), P("parts", "tensor")),
        check_vma=False,
    )
```

```python
import functools

import jax
import jax.numpy as jnp
from jax import lax
from jax.experimental import pallas as pl
from jax.experimental.pallas import tpu as pltpu
from jax.sharding import PartitionSpec as P

RANK = 64
NUM_DIR = 40
WIDE = RANK * NUM_DIR
MESH = pl.DeviceIdType.MESH
F32 = jnp.float32
BF16 = jnp.bfloat16
NT = (((1,), (1,)), ((), ()))
TN = (((0,), (0,)), ((), ()))
NN = (((1,), (0,)), ((), ()))
PAD = 16
CHUNKS = 4


def dot(lhs, rhs, dims, **kw):
    return lax.dot_general(lhs, rhs, dims, preferred_element_type=F32, **kw)


def iota(shape, axis):
    return lax.broadcasted_iota(jnp.int32, shape, axis)


def direction_table(segment_ids, segment_dirs):
    seg_hot = (
        segment_ids[:, None] == jnp.arange(segment_dirs.shape[0], dtype=jnp.int32)[None, :]
    ).astype(F32)
    dir_hot = (segment_dirs[:, None] == jnp.arange(NUM_DIR, dtype=jnp.int32)[None, :]).astype(F32)
    return jnp.dot(seg_hot, dir_hot, precision=lax.Precision.HIGHEST)


def select_rank(wide, onehot):
    count = wide.shape[0]
    return jnp.sum(wide.reshape(count, NUM_DIR, RANK) * onehot[:, :, None], axis=1)


def spread_rank(low, onehot):
    count = low.shape[0]
    return (
        (0.5 * onehot[:, :, None] * low[:, None, :]).reshape(count, NUM_DIR * RANK).astype(BF16)
    )


def per_device_plain(
    cotangent, hidden, down_weight, adapter_in, adapter_out, segment_ids, segment_dirs
):
    onehot = direction_table(segment_ids, segment_dirs)
    width_share = adapter_out.shape[1]
    shards = cotangent.shape[1] // width_share
    own = cotangent.shape[0]
    full_rows = lax.all_gather(cotangent, "tensor", axis=0, tiled=True)
    pieces = cotangent.reshape(own, shards, width_share).transpose(1, 0, 2)
    columns = lax.all_to_all(pieces, "tensor", 0, 0, tiled=True).reshape(shards * own, width_share)
    wide_u = dot(columns, adapter_out, NT)
    wide_v = dot(hidden, adapter_in, NN)
    part = jnp.concatenate([select_rank(wide_u, onehot), select_rank(wide_v, onehot)], axis=1)
    low = lax.psum(part, "tensor")
    spread_u = spread_rank(low[:, :RANK], onehot)
    spread_v = spread_rank(low[:, RANK:], onehot)
    grad_in = dot(hidden, spread_u, TN)
    grad_out = dot(spread_v, columns, TN)
    base = dot(full_rows, down_weight, NT)
    extra = dot(spread_u, adapter_in, NT)
    return ((base + extra).astype(BF16), grad_in, grad_out)


def number_columns(place, number_row):
    ones = jnp.ones((place.shape[1], 128), BF16)
    return dot((place * (number_row + 1.0)).astype(BF16), ones, NN) - 1.0


def padded_place(own, tokens, rows, flip):
    shape = (tokens, rows) if flip else (rows, tokens)
    row, token = (iota(shape, 1), iota(shape, 0)) if flip else (iota(shape, 0), iota(shape, 1))
    inside = lax.rem(row, PAD)
    return ((token == own * (row // PAD) + inside) & (inside < own)).astype(F32)


def half_shift(shape):
    return (iota(shape, 1) >= RANK).astype(F32)


def main_kernel(
    cot_hbm, hid_hbm, dw_hbm, ain_hbm, aout_hbm, ids_ref, dirs_ref,
    acc_hbm, low_hbm, cols_hbm,
    cot, gat, fourth, dw, ain, aout, hid, acc, wide_cols, lpart, rpart, low, perm,
    ld_sem, st_sem, gs_sem, gr_sem, sib_sem, x_sem, cs_sem, chain_sem,
):
    own, width = cot_hbm.shape
    tokens, ff = hid_hbm.shape
    share = aout_hbm.shape[1]
    shards = width // share
    rows = shards * PAD
    quarter = width // 4
    step = quarter // CHUNKS

    p = lax.axis_index("parts")
    me = lax.axis_index("tensor")
    z, x, c = me // 4, lax.rem(me // 2, 2), lax.rem(me, 2)
    zs = [z, z + 1 - 2 * lax.rem(z, 2), lax.rem(z + 2, 4), 3 - z]

    def index(zz, xx, cc):
        return zz * 4 + xx * 2 + cc

    sib = index(z, x, 1 - c)
    xnb = index(z, 1 - x, c)
    z1, z2, z3 = (index(zs[k], x, c) for k in (1, 2, 3))

    def dev(i):
        return (p, i)

    bar = pltpu.get_barrier_semaphore()
    for nb in (sib, xnb, z1, z2, z3):
        pl.semaphore_signal(bar, inc=1, device_id=dev(nb), device_id_type=MESH)

    ld_cot = pltpu.make_async_copy(cot_hbm, cot, ld_sem.at[0])
    ld_hid = pltpu.make_async_copy(hid_hbm, hid, ld_sem.at[1])
    ld_cot.start()
    ld_hid.start()
    n_ain = WIDE // 512
    ld_ain = []
    for i in range(n_ain):
        cut = pl.ds(512 * i, 512)
        ld_ain.append(
            pltpu.make_async_copy(ain_hbm.at[:, cut], ain.at[:, cut], ld_sem.at[2 + i])
        )
        ld_ain[-1].start()
    ld_aout = pltpu.make_async_copy(aout_hbm, aout, ld_sem.at[2 + n_ain])
    ld_aout.start()
    for q in range(CHUNKS):
        for j in range(4):
            cut = pl.ds(quarter * j + step * q, step)
            pltpu.make_async_copy(
                dw_hbm.at[:, cut], dw.at[:, cut], ld_sem.at[3 + n_ain + q]
            ).start()

    def wait_dw(q):
        cut = pl.ds(quarter * q, quarter)
        pltpu.make_async_copy(dw_hbm.at[:, cut], dw.at[:, cut], ld_sem.at[3 + n_ain + q]).wait()

    def rows_of(b):
        return pl.ds(pl.multiple_of(b * PAD, PAD), PAD)

    def piece(b, q):
        return gat.at[:, rows_of(b), pl.ds(step * q, step)]

    def send(b, q, to, sem, recv):
        pltpu.make_async_remote_copy(
            src_ref=piece(b, q), dst_ref=piece(b, q), send_sem=sem, recv_sem=recv,
            device_id=dev(to), device_id_type=MESH,
        ).start()

    def arrived(b, q, sem):
        pltpu.make_async_copy(piece(b, q), piece(b, q), sem).wait()

    def col_block(k):
        return index(zs[k], x, c)

    def x_block(k):
        return index(zs[k], 1 - x, c)

    def send_own(q):
        send(me, q, xnb, gs_sem.at[0], x_sem.at[q])
        for k, to in ((1, z1), (2, z2), (3, z3)):
            send(me, q, to, gs_sem.at[0], gr_sem.at[(k - 1) * CHUNKS + q])
        send(me, q, sib, gs_sem.at[0], sib_sem.at[q])

    def take_column(k, q):
        b = col_block(k)
        arrived(b, q, gr_sem.at[(k - 1) * CHUNKS + q])
        send(b, q, xnb, gs_sem.at[0], x_sem.at[k * CHUNKS + q])
        send(b, q, sib, gs_sem.at[0], sib_sem.at[q])

    def take_x(k, q):
        b = x_block(k)
        arrived(b, q, x_sem.at[k * CHUNKS + q])
        send(b, q, sib, gs_sem.at[0], sib_sem.at[q])

    def take_sib(q):
        half = gat.at[:, pl.ds(0, rows // 2), pl.ds(step * q, step)]
        pltpu.make_async_copy(half, half, sib_sem.at[q]).wait()

    chain = (z1, z2, xnb, sib)

    def greet(i):
        pl.semaphore_signal(chain_sem.at[i], inc=1, device_id=dev(chain[i]), device_id_type=MESH)

    def greeted(i):
        pl.semaphore_wait(chain_sem.at[i], 1)

    ld_cot.wait()
    cot32 = cot[...].astype(F32)
    gap = PAD - own
    for j in range(3):
        tile = jnp.concatenate(
            [
                cot32[:, quarter * j : quarter * (j + 1)],
                cot32[gap * j : gap * (j + 1), 3 * quarter :],
            ],
            axis=0,
        )
        gat[j, rows_of(me), :] = tile.astype(BF16)
    pl.semaphore_wait(bar, 5)
    for q in range(CHUNKS):
        send_own(q)
    greet(0)

    dir_row = jnp.zeros((1, tokens), F32)
    ids = ids_ref[...]
    for s in range(dirs_ref.shape[0]):
        dir_row = jnp.where(ids == s, dirs_ref[s].astype(F32), dir_row)
    pad_place = padded_place(own, tokens, rows, False)
    dense_place = (iota((tokens, tokens), 0) == iota((tokens, tokens), 1)).astype(F32)
    dirs_dense = number_columns(dense_place, dir_row) - half_shift((tokens, 128))
    dirs_pad = number_columns(pad_place, dir_row) - half_shift((rows, 128))
    for j in range(3):
        a, b = iota((rows, rows), 0), iota((rows, rows), 1)
        ra, rb = lax.rem(a, PAD), lax.rem(b, PAD)
        hit = (a // PAD == b // PAD) & (ra // gap == j) & (rb - own == ra - gap * j)
        perm[j] = hit.astype(BF16)

    def pick(total, wide, where, first):
        for i in range(wide.shape[1] // 128):
            total = total + jnp.where(
                where == float(first + 2 * i), wide[:, 128 * i : 128 * (i + 1)], 0.0
            )
        return total

    ld_hid.wait()
    tot_v = jnp.zeros((tokens, 128), F32)
    for i in range(n_ain):
        ld_ain[i].wait()
        wide = dot(hid[...], ain[:, 512 * i : 512 * (i + 1)], NN)
        tot_v = pick(tot_v, wide, dirs_dense, 8 * i)
        if i == 1:
            greeted(0)
            greet(1)
            take_column(1, 0)
            take_column(2, 0)
    take_column(3, 0)
    take_column(1, 1)
    tot_v = dot(pad_place, tot_v, NN, precision=lax.Precision.HIGHEST)
    v = tot_v + pltpu.roll(tot_v, RANK, 1)

    greeted(1)
    greet(2)
    take_x(0, 0)
    take_x(1, 0)
    take_x(2, 0)
    take_x(3, 0)
    take_column(2, 1)
    take_column(3, 1)
    greeted(2)
    greet(3)
    ld_aout.wait()

    def assemble(q):
        cut = pl.ds(step * q, step)
        total = dot(perm[0], gat[0, :, cut], NN)
        total += dot(perm[1], gat[1, :, cut], NN)
        total += dot(perm[2], gat[2, :, cut], NN)
        fourth[:, cut] = total.astype(BF16)

    tile = ff // 2

    def base(q, h):
        r = pl.ds(tile * h, tile)
        total = acc[r, :] if q > 0 else None
        for j in range(4):
            cut = slice(quarter * j + step * q, quarter * j + step * (q + 1))
            rhs = (fourth if j == 3 else gat.at[j])[:, step * q : step * (q + 1)]
            add = dot(dw[r, cut], rhs, NT)
            total = add if total is None else total + add
        acc[r, :] = total

    def stage(q):
        take_sib(q)
        wait_dw(q)
        assemble(q)

    take_column(1, 2)
    take_column(2, 2)
    take_column(3, 2)
    take_x(0, 1)
    take_x(1, 1)
    take_x(2, 1)
    take_x(3, 1)
    stage(0)
    base(0, 0)
    take_column(1, 3)
    take_column(2, 3)
    take_column(3, 3)
    take_x(0, 2)
    take_x(1, 2)
    base(0, 1)
    greeted(3)
    take_x(2, 2)
    take_x(3, 2)
    stage(1)
    base(1, 0)
    take_x(0, 3)
    take_x(1, 3)
    stage(2)
    take_x(2, 3)
    take_x(3, 3)
    stage(3)

    own_cols = pl.ds(pl.multiple_of((2 * x + c) * share, share), share)

    @pl.when(z < 3)
    def _():
        wide_cols[...] = gat[lax.rem(z, 3), :, own_cols]

    @pl.when(z == 3)
    def _():
        wide_cols[...] = fourth[:, own_cols]

    tot_u = jnp.zeros((rows, 128), F32)
    for i in range(n_ain):
        wide = dot(wide_cols[...], aout[512 * i : 512 * (i + 1), :], NT)
        tot_u = pick(tot_u, wide, dirs_pad, 8 * i)
    u = tot_u + pltpu.roll(tot_u, RANK, 1)
    lpart[...] = jnp.where(iota((rows, 128), 1) < RANK, u, v).astype(BF16)
    for i in range(1, shards):
        d = lax.rem(me + i, shards)
        pltpu.make_async_remote_copy(
            src_ref=lpart.at[rows_of(d), :], dst_ref=rpart.at[me],
            send_sem=cs_sem.at[0], recv_sem=cs_sem.at[1],
            device_id=dev(d), device_id_type=MESH,
        ).start()
    rpart[me] = lpart[rows_of(me), :]
    put_cols = pltpu.make_async_copy(wide_cols, cols_hbm, st_sem.at[0])
    put_cols.start()
    base(1, 1)
    base(2, 0)
    pieces = rpart.at[pl.ds(0, shards - 1)]
    pltpu.make_async_copy(pieces, pieces, cs_sem.at[1]).wait()
    summed = rpart[0].astype(F32)
    for i in range(1, shards):
        summed = summed + rpart[i].astype(F32)
    low[rows_of(me), :] = (0.5 * summed).astype(BF16)
    for i in range(1, shards):
        d = lax.rem(me + i, shards)
        pltpu.make_async_remote_copy(
            src_ref=low.at[rows_of(me), :], dst_ref=low.at[rows_of(me), :],
            send_sem=cs_sem.at[2], recv_sem=cs_sem.at[3],
            device_id=dev(d), device_id_type=MESH,
        ).start()
    base(2, 1)
    base(3, 0)
    base(3, 1)
    put_acc = pltpu.make_async_copy(acc, acc_hbm, st_sem.at[2])
    put_acc.start()
    known = low.at[pl.ds(0, rows - PAD), :]
    pltpu.make_async_copy(known, known, cs_sem.at[3]).wait()
    put_low = pltpu.make_async_copy(low, low_hbm, st_sem.at[1])
    put_low.start()

    def left(units, sem):
        sent = gat.at[:, pl.ds(0, units * PAD), :]
        pltpu.make_async_copy(sent, sent, sem).wait()

    left(15, gs_sem.at[0])
    pltpu.make_async_copy(pieces, pieces, cs_sem.at[0]).wait()
    pltpu.make_async_copy(known, known, cs_sem.at[2]).wait()
    for put in (put_cols, put_acc, put_low):
        put.wait()


def write_kernel(
    own, acc_in, low_in, cols_in, hid_in, ain_in, ids_ref, dirs_ref,
    gh_hbm, gin_hbm, gout_hbm,
    low, cols, hid, acc, ain, gh, gin, gout, zero, ld_sem, ain_sem, in_sem, out_sem,
):
    tokens, ff = hid_in.shape
    rows = low_in.shape[0]
    share = cols_in.shape[1]
    segs = dirs_ref.shape[0]
    pairs = NUM_DIR // 2
    loads = [
        pltpu.make_async_copy(src, dst, ld_sem.at[i])
        for i, (src, dst) in enumerate(((low_in, low), (hid_in, hid), (cols_in, cols), (acc_in, acc)))
    ]
    for load in loads:
        load.start()
    zero[...] = jnp.zeros_like(zero)

    def in_part(i):
        return gin_hbm.at[:, pl.ds(128 * i, 128)]

    def out_part(i):
        return gout_hbm.at[pl.ds(128 * i, 128), :]

    used = []
    for i in range(pairs):
        hit = dirs_ref[0] // 2 == i
        for s in range(1, segs):
            hit = hit | (dirs_ref[s] // 2 == i)
        used.append(hit)

    def ain_load(i):
        return pltpu.make_async_copy(ain_in.at[:, pl.ds(128 * i, 128)], ain.at[i], ain_sem.at[i])

    for i in range(pairs):
        pl.when(used[i])(ain_load(i).start)
    for i in range(pairs):

        @pl.when(jnp.logical_not(used[i]))
        def _():
            pltpu.make_async_copy(zero, in_part(i), in_sem.at[i]).start()
            for n in range(share // 128):
                pltpu.make_async_copy(
                    zero.at[pl.ds(0, 128), :],
                    gout_hbm.at[pl.ds(128 * i, 128), pl.ds(128 * n, 128)],
                    out_sem.at[i],
                ).start()

    dir_row = jnp.zeros((1, tokens), F32)
    ids = ids_ref[...]
    for s in range(segs):
        dir_row = jnp.where(ids == s, dirs_ref[s].astype(F32), dir_row)
    pad_place = padded_place(own, tokens, rows, False)
    dense_place = (iota((tokens, tokens), 0) == iota((tokens, tokens), 1)).astype(F32)
    dirs_dense = number_columns(dense_place, dir_row) - half_shift((tokens, 128))
    dirs_pad = number_columns(pad_place, dir_row) - half_shift((rows, 128))
    place = padded_place(own, tokens, rows, True).astype(BF16)
    loads[0].wait()
    dense = dot(place, low[...], NN)
    u_twice = jnp.where(iota((tokens, 128), 1) < RANK, dense, pltpu.roll(dense, RANK, 1))
    both = low[...].astype(F32)
    v_twice = jnp.where(iota((rows, 128), 1) < RANK, pltpu.roll(both, RANK, 1), both)
    u_pad = jnp.where(iota((rows, 128), 1) < RANK, both, pltpu.roll(both, RANK, 1))
    for load in loads[1:]:
        load.wait()
    for i in range(pairs):

        @pl.when(used[i])
        def _():
            spread_u = jnp.where(dirs_dense == float(2 * i), u_twice, 0.0).astype(BF16)
            gin[:, 128 * i : 128 * (i + 1)] = dot(hid[...], spread_u, TN)
            pltpu.make_async_copy(
                gin.at[:, pl.ds(128 * i, 128)], in_part(i), in_sem.at[i]
            ).start()
            spread_v = jnp.where(dirs_pad == float(2 * i), v_twice, 0.0).astype(BF16)
            gout[128 * i : 128 * (i + 1), :] = dot(spread_v, cols[...], TN)
            pltpu.make_async_copy(
                gout.at[pl.ds(128 * i, 128), :], out_part(i), out_sem.at[i]
            ).start()
            ain_load(i).wait()
            spread_pad = jnp.where(dirs_pad == float(2 * i), u_pad, 0.0).astype(BF16)
            acc[...] += dot(ain[i], spread_pad, NT)

    gh[...] = dot(place, acc[...].astype(BF16), NT).astype(BF16)
    put_gh = pltpu.make_async_copy(gh, gh_hbm, ld_sem.at[4])
    put_gh.start()
    put_gh.wait()
    for i in range(pairs):
        pltpu.make_async_copy(gin.at[:, pl.ds(128 * i, 128)], in_part(i), in_sem.at[i]).wait()
        pltpu.make_async_copy(gout.at[pl.ds(128 * i, 128), :], out_part(i), out_sem.at[i]).wait()


def per_device(cotangent, hidden, down_weight, adapter_in, adapter_out, segment_ids, segment_dirs):
    own, width = cotangent.shape
    tokens, ff = hidden.shape
    share = adapter_out.shape[1]
    shards = width // share
    rows = shards * PAD
    ids = segment_ids.reshape(1, tokens)
    any_space = pl.BlockSpec(memory_space=pl.ANY)
    vmem = pl.BlockSpec(memory_space=pltpu.VMEM)
    smem = pl.BlockSpec(memory_space=pltpu.SMEM)
    acc, low, cols = pl.pallas_call(
        main_kernel,
        out_shape=(
            jax.ShapeDtypeStruct((ff, rows), F32),
            jax.ShapeDtypeStruct((rows, 128), BF16),
            jax.ShapeDtypeStruct((rows, share), BF16),
        ),
        in_specs=[any_space] * 5 + [vmem, smem],
        out_specs=(any_space,) * 3,
        scratch_shapes=[
            pltpu.VMEM((own, width), BF16),
            pltpu.VMEM((3, rows, width // 4), BF16),
            pltpu.VMEM((rows, width // 4), BF16),
            pltpu.VMEM((ff, width), BF16),
            pltpu.VMEM((ff, WIDE), BF16),
            pltpu.VMEM((WIDE, share), BF16),
            pltpu.VMEM((tokens, ff), BF16),
            pltpu.VMEM((ff, rows), F32),
            pltpu.VMEM((rows, share), BF16),
            pltpu.VMEM((rows, 128), BF16),
            pltpu.VMEM((shards, PAD, 128), BF16),
            pltpu.VMEM((rows, 128), BF16),
            pltpu.VMEM((3, rows, rows), BF16),
            pltpu.SemaphoreType.DMA((3 + WIDE // 512 + CHUNKS,)),
            pltpu.SemaphoreType.DMA((3,)),
            pltpu.SemaphoreType.DMA((1,)),
            pltpu.SemaphoreType.DMA((3 * CHUNKS,)),
            pltpu.SemaphoreType.DMA((CHUNKS,)),
            pltpu.SemaphoreType.DMA((4 * CHUNKS,)),
            pltpu.SemaphoreType.DMA((4,)),
            pltpu.SemaphoreType.REGULAR((4,)),
        ],
        compiler_params=pltpu.CompilerParams(
            collective_id=0, has_side_effects=True, vmem_limit_bytes=60 << 20
        ),
        cost_estimate=pl.CostEstimate(
            flops=2 * rows * ff * width, bytes_accessed=2 * ff * (width + WIDE), transcendentals=0
        ),
    )(cotangent, hidden, down_weight, adapter_in, adapter_out, ids, segment_dirs)
    return pl.pallas_call(
        functools.partial(write_kernel, own),
        out_shape=(
            jax.ShapeDtypeStruct((tokens, ff), BF16),
            jax.ShapeDtypeStruct((ff, WIDE), F32),
            jax.ShapeDtypeStruct((WIDE, share), F32),
        ),
        in_specs=[any_space] * 5 + [vmem, smem],
        out_specs=(any_space,) * 3,
        scratch_shapes=[
            pltpu.VMEM((rows, 128), BF16),
            pltpu.VMEM((rows, share), BF16),
            pltpu.VMEM((tokens, ff), BF16),
            pltpu.VMEM((ff, rows), F32),
            pltpu.VMEM((NUM_DIR // 2, ff, 128), BF16),
            pltpu.VMEM((tokens, ff), BF16),
            pltpu.VMEM((ff, WIDE), F32),
            pltpu.VMEM((WIDE, share), F32),
            pltpu.VMEM((ff, 128), F32),
            pltpu.SemaphoreType.DMA((5,)),
            pltpu.SemaphoreType.DMA((NUM_DIR // 2,)),
            pltpu.SemaphoreType.DMA((NUM_DIR // 2,)),
            pltpu.SemaphoreType.DMA((NUM_DIR // 2,)),
        ],
        compiler_params=pltpu.CompilerParams(vmem_limit_bytes=60 << 20),
        cost_estimate=pl.CostEstimate(
            flops=2 * tokens * ff * WIDE, bytes_accessed=4 * WIDE * (ff + share), transcendentals=0
        ),
    )(acc, low, cols, hidden, adapter_in, ids, segment_dirs)


def solution(mesh):
    def body(cotangent, hidden, *rest):
        own, width = cotangent.shape
        ff = hidden.shape[1]
        share = width // mesh.shape["tensor"]
        fits = (
            mesh.shape["tensor"] == 16
            and own == 12
            and hidden.shape[0] == 16 * own
            and width % (4 * CHUNKS * 128) == 0
            and share % 128 == 0
            and ff % 256 == 0
        )
        return (per_device if fits else per_device_plain)(cotangent, hidden, *rest)

    return jax.shard_map(
        body,
        mesh=mesh,
        in_specs=(
            P(("parts", "tensor"), None),
            P("parts", "tensor"),
            P("tensor", None),
            P("tensor", None),
            P(None, "tensor"),
            P("parts"),
            P("parts"),
        ),
        out_specs=(P("parts", "tensor"), P(("parts", "tensor"), None), P("parts", "tensor")),
        check_vma=False,
    )
```

```python
import functools

import jax
import jax.numpy as jnp
from jax import lax
from jax.experimental import pallas as pl
from jax.experimental.pallas import tpu as pltpu
from jax.sharding import PartitionSpec as P

RANK = 64
NUM_DIR = 40
WIDE = RANK * NUM_DIR
MESH = pl.DeviceIdType.MESH
F32 = jnp.float32
BF16 = jnp.bfloat16
NT = (((1,), (1,)), ((), ()))
TN = (((0,), (0,)), ((), ()))
NN = (((1,), (0,)), ((), ()))
PAD = 16
CHUNKS = 4


def dot(lhs, rhs, dims, **kw):
    return lax.dot_general(lhs, rhs, dims, preferred_element_type=F32, **kw)


def iota(shape, axis):
    return lax.broadcasted_iota(jnp.int32, shape, axis)


def direction_table(segment_ids, segment_dirs):
    seg_hot = (
        segment_ids[:, None] == jnp.arange(segment_dirs.shape[0], dtype=jnp.int32)[None, :]
    ).astype(F32)
    dir_hot = (segment_dirs[:, None] == jnp.arange(NUM_DIR, dtype=jnp.int32)[None, :]).astype(F32)
    return jnp.dot(seg_hot, dir_hot, precision=lax.Precision.HIGHEST)


def select_rank(wide, onehot):
    count = wide.shape[0]
    return jnp.sum(wide.reshape(count, NUM_DIR, RANK) * onehot[:, :, None], axis=1)


def spread_rank(low, onehot):
    count = low.shape[0]
    return (
        (0.5 * onehot[:, :, None] * low[:, None, :]).reshape(count, NUM_DIR * RANK).astype(BF16)
    )


def per_device_plain(
    cotangent, hidden, down_weight, adapter_in, adapter_out, segment_ids, segment_dirs
):
    onehot = direction_table(segment_ids, segment_dirs)
    width_share = adapter_out.shape[1]
    shards = cotangent.shape[1] // width_share
    own = cotangent.shape[0]
    full_rows = lax.all_gather(cotangent, "tensor", axis=0, tiled=True)
    pieces = cotangent.reshape(own, shards, width_share).transpose(1, 0, 2)
    columns = lax.all_to_all(pieces, "tensor", 0, 0, tiled=True).reshape(shards * own, width_share)
    wide_u = dot(columns, adapter_out, NT)
    wide_v = dot(hidden, adapter_in, NN)
    part = jnp.concatenate([select_rank(wide_u, onehot), select_rank(wide_v, onehot)], axis=1)
    low = lax.psum(part, "tensor")
    spread_u = spread_rank(low[:, :RANK], onehot)
    spread_v = spread_rank(low[:, RANK:], onehot)
    grad_in = dot(hidden, spread_u, TN)
    grad_out = dot(spread_v, columns, TN)
    base = dot(full_rows, down_weight, NT)
    extra = dot(spread_u, adapter_in, NT)
    return ((base + extra).astype(BF16), grad_in, grad_out)


def number_columns(place, number_row):
    ones = jnp.ones((place.shape[1], 128), BF16)
    return dot((place * (number_row + 1.0)).astype(BF16), ones, NN) - 1.0


def padded_place(own, tokens, rows, flip):
    shape = (tokens, rows) if flip else (rows, tokens)
    row, token = (iota(shape, 1), iota(shape, 0)) if flip else (iota(shape, 0), iota(shape, 1))
    inside = lax.rem(row, PAD)
    return ((token == own * (row // PAD) + inside) & (inside < own)).astype(F32)


def half_shift(shape):
    return (iota(shape, 1) >= RANK).astype(F32)


def main_kernel(
    cot_hbm, hid_hbm, dw_hbm, ain_hbm, aout_hbm, ids_ref, dirs_ref,
    acc_hbm, low_hbm, cols_hbm,
    cot, gat, fourth, dw, ain, aout, hid, acc, wide_cols, lpart, rpart, low, perm,
    ld_sem, st_sem, gs_sem, gr_sem, sib_sem, x_sem, cs_sem, chain_sem,
):
    own, width = cot_hbm.shape
    tokens, ff = hid_hbm.shape
    share = aout_hbm.shape[1]
    shards = width // share
    rows = shards * PAD
    quarter = width // 4
    step = quarter // CHUNKS

    p = lax.axis_index("parts")
    me = lax.axis_index("tensor")
    z, x, c = me // 4, lax.rem(me // 2, 2), lax.rem(me, 2)
    zs = [z, z + 1 - 2 * lax.rem(z, 2), lax.rem(z + 2, 4), 3 - z]

    def index(zz, xx, cc):
        return zz * 4 + xx * 2 + cc

    sib = index(z, x, 1 - c)
    xnb = index(z, 1 - x, c)
    z1, z2, z3 = (index(zs[k], x, c) for k in (1, 2, 3))

    def dev(i):
        return (p, i)

    bar = pltpu.get_barrier_semaphore()
    for nb in (sib, xnb, z1, z2, z3):
        pl.semaphore_signal(bar, inc=1, device_id=dev(nb), device_id_type=MESH)

    ld_cot = pltpu.make_async_copy(cot_hbm, cot, ld_sem.at[0])
    ld_hid = pltpu.make_async_copy(hid_hbm, hid, ld_sem.at[1])
    ld_cot.start()
    ld_hid.start()
    n_ain = WIDE // 512
    ld_ain = []
    for i in range(n_ain):
        cut = pl.ds(512 * i, 512)
        ld_ain.append(
            pltpu.make_async_copy(ain_hbm.at[:, cut], ain.at[:, cut], ld_sem.at[2 + i])
        )
        ld_ain[-1].start()
    ld_aout = pltpu.make_async_copy(aout_hbm, aout, ld_sem.at[2 + n_ain])
    ld_aout.start()
    for q in range(CHUNKS):
        for j in range(4):
            cut = pl.ds(quarter * j + step * q, step)
            pltpu.make_async_copy(
                dw_hbm.at[:, cut], dw.at[:, cut], ld_sem.at[3 + n_ain + q]
            ).start()

    def wait_dw(q):
        cut = pl.ds(quarter * q, quarter)
        pltpu.make_async_copy(dw_hbm.at[:, cut], dw.at[:, cut], ld_sem.at[3 + n_ain + q]).wait()

    def rows_of(b):
        return pl.ds(pl.multiple_of(b * PAD, PAD), PAD)

    def piece(b, q):
        return gat.at[:, rows_of(b), pl.ds(step * q, step)]

    def send(b, q, to, sem, recv):
        pltpu.make_async_remote_copy(
            src_ref=piece(b, q), dst_ref=piece(b, q), send_sem=sem, recv_sem=recv,
            device_id=dev(to), device_id_type=MESH,
        ).start()

    def arrived(b, q, sem):
        pltpu.make_async_copy(piece(b, q), piece(b, q), sem).wait()

    def col_block(k):
        return index(zs[k], x, c)

    def x_block(k):
        return index(zs[k], 1 - x, c)

    def send_own(q):
        send(me, q, xnb, gs_sem.at[0], x_sem.at[q])
        for k, to in ((1, z1), (2, z2), (3, z3)):
            send(me, q, to, gs_sem.at[0], gr_sem.at[(k - 1) * CHUNKS + q])
        send(me, q, sib, gs_sem.at[0], sib_sem.at[q])

    def take_column(k, q):
        b = col_block(k)
        arrived(b, q, gr_sem.at[(k - 1) * CHUNKS + q])
        send(b, q, xnb, gs_sem.at[0], x_sem.at[k * CHUNKS + q])
        send(b, q, sib, gs_sem.at[0], sib_sem.at[q])

    def take_x(k, q):
        b = x_block(k)
        arrived(b, q, x_sem.at[k * CHUNKS + q])
        send(b, q, sib, gs_sem.at[0], sib_sem.at[q])

    def take_sib(q):
        half = gat.at[:, pl.ds(0, rows // 2), pl.ds(step * q, step)]
        pltpu.make_async_copy(half, half, sib_sem.at[q]).wait()

    chain = (z1, z2, xnb, sib)

    def greet(i):
        pl.semaphore_signal(chain_sem.at[i], inc=1, device_id=dev(chain[i]), device_id_type=MESH)

    def greeted(i):
        pl.semaphore_wait(chain_sem.at[i], 1)

    ld_cot.wait()
    cot32 = cot[...].astype(F32)
    gap = PAD - own
    for j in range(3):
        tile = jnp.concatenate(
            [
                cot32[:, quarter * j : quarter * (j + 1)],
                cot32[gap * j : gap * (j + 1), 3 * quarter :],
            ],
            axis=0,
        )
        gat[j, rows_of(me), :] = tile.astype(BF16)
    pl.semaphore_wait(bar, 5)
    for q in range(CHUNKS):
        send_own(q)
    greet(0)

    dir_row = jnp.zeros((1, tokens), F32)
    ids = ids_ref[...]
    for s in range(dirs_ref.shape[0]):
        dir_row = jnp.where(ids == s, dirs_ref[s].astype(F32), dir_row)
    pad_place = padded_place(own, tokens, rows, False)
    dense_place = (iota((tokens, tokens), 0) == iota((tokens, tokens), 1)).astype(F32)
    dirs_dense = number_columns(dense_place, dir_row) - half_shift((tokens, 128))
    dirs_pad = number_columns(pad_place, dir_row) - half_shift((rows, 128))
    for j in range(3):
        a, b = iota((rows, rows), 0), iota((rows, rows), 1)
        ra, rb = lax.rem(a, PAD), lax.rem(b, PAD)
        hit = (a // PAD == b // PAD) & (ra // gap == j) & (rb - own == ra - gap * j)
        perm[j] = hit.astype(BF16)

    def pick(total, wide, where, first):
        for i in range(wide.shape[1] // 128):
            total = total + jnp.where(
                where == float(first + 2 * i), wide[:, 128 * i : 128 * (i + 1)], 0.0
            )
        return total

    ld_hid.wait()
    tot_v = jnp.zeros((tokens, 128), F32)
    for i in range(n_ain):
        ld_ain[i].wait()
        wide = dot(hid[...], ain[:, 512 * i : 512 * (i + 1)], NN)
        tot_v = pick(tot_v, wide, dirs_dense, 8 * i)
        if i == 1:
            greeted(0)
            greet(1)
            take_column(1, 0)
            take_column(2, 0)
    take_column(3, 0)
    take_column(1, 1)
    tot_v = dot(pad_place, tot_v, NN, precision=lax.Precision.HIGHEST)
    v = tot_v + pltpu.roll(tot_v, RANK, 1)

    greeted(1)
    greet(2)
    take_x(0, 0)
    take_x(1, 0)
    take_x(2, 0)
    take_x(3, 0)
    take_column(2, 1)
    take_column(3, 1)
    greeted(2)
    greet(3)
    ld_aout.wait()

    def assemble(q):
        cut = pl.ds(step * q, step)
        total = dot(perm[0], gat[0, :, cut], NN)
        total += dot(perm[1], gat[1, :, cut], NN)
        total += dot(perm[2], gat[2, :, cut], NN)
        fourth[:, cut] = total.astype(BF16)

    tile = ff // 2

    def base(q, h):
        r = pl.ds(tile * h, tile)
        total = acc[r, :] if q > 0 else None
        for j in range(4):
            cut = slice(quarter * j + step * q, quarter * j + step * (q + 1))
            rhs = (fourth if j == 3 else gat.at[j])[:, step * q : step * (q + 1)]
            add = dot(dw[r, cut], rhs, NT)
            total = add if total is None else total + add
        acc[r, :] = total

    def stage(q):
        take_sib(q)
        wait_dw(q)
        assemble(q)

    take_column(1, 2)
    take_column(2, 2)
    take_column(3, 2)
    take_x(0, 1)
    take_x(1, 1)
    take_x(2, 1)
    take_x(3, 1)
    take_column(1, 3)
    take_column(2, 3)
    take_column(3, 3)
    stage(0)
    base(0, 0)
    greeted(3)
    take_x(0, 2)
    take_x(1, 2)
    take_x(2, 2)
    take_x(3, 2)
    base(0, 1)
    take_x(0, 3)
    take_x(1, 3)
    stage(1)
    stage(2)
    take_x(2, 3)
    take_x(3, 3)
    stage(3)

    own_cols = pl.ds(pl.multiple_of((2 * x + c) * share, share), share)

    @pl.when(z < 3)
    def _():
        wide_cols[...] = gat[lax.rem(z, 3), :, own_cols]

    @pl.when(z == 3)
    def _():
        wide_cols[...] = fourth[:, own_cols]

    tot_u = jnp.zeros((rows, 128), F32)
    for i in range(n_ain):
        wide = dot(wide_cols[...], aout[512 * i : 512 * (i + 1), :], NT)
        tot_u = pick(tot_u, wide, dirs_pad, 8 * i)
    u = tot_u + pltpu.roll(tot_u, RANK, 1)
    lpart[...] = jnp.where(iota((rows, 128), 1) < RANK, u, v).astype(BF16)
    for i in range(1, shards):
        d = lax.rem(me + i, shards)
        pltpu.make_async_remote_copy(
            src_ref=lpart.at[rows_of(d), :], dst_ref=rpart.at[me],
            send_sem=cs_sem.at[0], recv_sem=cs_sem.at[1],
            device_id=dev(d), device_id_type=MESH,
        ).start()
    rpart[me] = lpart[rows_of(me), :]
    put_cols = pltpu.make_async_copy(wide_cols, cols_hbm, st_sem.at[0])
    put_cols.start()
    base(1, 0)
    base(1, 1)
    base(2, 0)
    pieces = rpart.at[pl.ds(0, shards - 1)]
    pltpu.make_async_copy(pieces, pieces, cs_sem.at[1]).wait()
    summed = rpart[0].astype(F32)
    for i in range(1, shards):
        summed = summed + rpart[i].astype(F32)
    low[rows_of(me), :] = (0.5 * summed).astype(BF16)
    for i in range(1, shards):
        d = lax.rem(me + i, shards)
        pltpu.make_async_remote_copy(
            src_ref=low.at[rows_of(me), :], dst_ref=low.at[rows_of(me), :],
            send_sem=cs_sem.at[2], recv_sem=cs_sem.at[3],
            device_id=dev(d), device_id_type=MESH,
        ).start()
    base(2, 1)
    base(3, 0)
    base(3, 1)
    put_acc = pltpu.make_async_copy(acc, acc_hbm, st_sem.at[2])
    put_acc.start()
    known = low.at[pl.ds(0, rows - PAD), :]
    pltpu.make_async_copy(known, known, cs_sem.at[3]).wait()
    put_low = pltpu.make_async_copy(low, low_hbm, st_sem.at[1])
    put_low.start()

    def left(units, sem):
        sent = gat.at[:, pl.ds(0, units * PAD), :]
        pltpu.make_async_copy(sent, sent, sem).wait()

    left(15, gs_sem.at[0])
    pltpu.make_async_copy(pieces, pieces, cs_sem.at[0]).wait()
    pltpu.make_async_copy(known, known, cs_sem.at[2]).wait()
    for put in (put_cols, put_acc, put_low):
        put.wait()


def write_kernel(
    own, acc_in, low_in, cols_in, hid_in, ain_in, ids_ref, dirs_ref,
    gh_hbm, gin_hbm, gout_hbm,
    low, cols, hid, acc, asel, gh, gin, gout, spread, spread_v, ld_sem, ain_sem, out_sem,
):
    tokens, ff = hid_in.shape
    rows = low_in.shape[0]
    segs = dirs_ref.shape[0]
    loads = [
        pltpu.make_async_copy(src, dst, ld_sem.at[i])
        for i, (src, dst) in enumerate(((low_in, low), (hid_in, hid), (cols_in, cols), (acc_in, acc)))
    ]
    for load in loads:
        load.start()
    for s in range(segs):
        start = pl.multiple_of((dirs_ref[s] // 2) * 128, 128)
        pltpu.make_async_copy(
            ain_in.at[:, pl.ds(start, 128)], asel.at[:, pl.ds(128 * s, 128)], ain_sem.at[s]
        ).start()
    dir_row = jnp.zeros((1, tokens), F32)
    ids = ids_ref[...]
    for s in range(segs):
        dir_row = jnp.where(ids == s, dirs_ref[s].astype(F32), dir_row)
    pad_place = padded_place(own, tokens, rows, False)
    dense_place = (iota((tokens, tokens), 0) == iota((tokens, tokens), 1)).astype(F32)
    dirs_dense = number_columns(dense_place, dir_row) - half_shift((tokens, 128))
    dirs_pad = number_columns(pad_place, dir_row) - half_shift((rows, 128))
    place = padded_place(own, tokens, rows, True).astype(BF16)
    loads[0].wait()
    dense = dot(place, low[...], NN)
    u_twice = jnp.where(iota((tokens, 128), 1) < RANK, dense, pltpu.roll(dense, RANK, 1))
    for i in range(NUM_DIR // 2):
        spread[:, 128 * i : 128 * (i + 1)] = jnp.where(
            dirs_dense == float(2 * i), u_twice, 0.0
        ).astype(BF16)
    loads[1].wait()
    puts = []

    def put(src, dst):
        puts.append(pltpu.make_async_copy(src, dst, out_sem.at[len(puts)]))
        puts[-1].start()

    tile = 256
    for i in range(ff // tile):
        r = pl.ds(tile * i, tile)
        gin[r, :] = dot(hid[:, tile * i : tile * (i + 1)], spread[...], TN)
        put(gin.at[r, :], gin_hbm.at[r, :])

    both = low[...].astype(F32)
    u_pad = jnp.where(iota((rows, 128), 1) < RANK, both, pltpu.roll(both, RANK, 1))
    v_pad = jnp.where(iota((rows, 128), 1) < RANK, pltpu.roll(both, RANK, 1), both)
    code = 2.0 * number_columns(pad_place, ids.astype(F32)) + half_shift((rows, 128))
    spread_pad = jnp.concatenate(
        [
            jnp.where(code == (2 * s + lax.rem(dirs_ref[s], 2)).astype(F32), u_pad, 0.0).astype(BF16)
            for s in range(segs)
        ],
        axis=1,
    )
    for s in range(segs):
        pltpu.make_async_copy(
            ain_in.at[:, pl.ds(0, 128)], asel.at[:, pl.ds(128 * s, 128)], ain_sem.at[s]
        ).wait()
    loads[3].wait()
    for h in range(2):
        r = pl.ds(ff // 2 * h, ff // 2)
        total = acc[r, :] + dot(asel[r, :], spread_pad, NT)
        gh[:, r] = dot(place, total.astype(BF16), NT).astype(BF16)
    put(gh, gh_hbm)
    for i in range(NUM_DIR // 2):
        spread_v[:, 128 * i : 128 * (i + 1)] = jnp.where(
            dirs_pad == float(2 * i), v_pad, 0.0
        ).astype(BF16)
    loads[2].wait()
    for i in range(WIDE // 512):
        r = pl.ds(512 * i, 512)
        gout[r, :] = dot(spread_v[:, 512 * i : 512 * (i + 1)], cols[...], TN)
        put(gout.at[r, :], gout_hbm.at[r, :])
    for copy in puts:
        copy.wait()


def per_device(cotangent, hidden, down_weight, adapter_in, adapter_out, segment_ids, segment_dirs):
    own, width = cotangent.shape
    tokens, ff = hidden.shape
    share = adapter_out.shape[1]
    shards = width // share
    rows = shards * PAD
    ids = segment_ids.reshape(1, tokens)
    any_space = pl.BlockSpec(memory_space=pl.ANY)
    vmem = pl.BlockSpec(memory_space=pltpu.VMEM)
    smem = pl.BlockSpec(memory_space=pltpu.SMEM)
    acc, low, cols = pl.pallas_call(
        main_kernel,
        out_shape=(
            jax.ShapeDtypeStruct((ff, rows), F32),
            jax.ShapeDtypeStruct((rows, 128), BF16),
            jax.ShapeDtypeStruct((rows, share), BF16),
        ),
        in_specs=[any_space] * 5 + [vmem, smem],
        out_specs=(any_space,) * 3,
        scratch_shapes=[
            pltpu.VMEM((own, width), BF16),
            pltpu.VMEM((3, rows, width // 4), BF16),
            pltpu.VMEM((rows, width // 4), BF16),
            pltpu.VMEM((ff, width), BF16),
            pltpu.VMEM((ff, WIDE), BF16),
            pltpu.VMEM((WIDE, share), BF16),
            pltpu.VMEM((tokens, ff), BF16),
            pltpu.VMEM((ff, rows), F32),
            pltpu.VMEM((rows, share), BF16),
            pltpu.VMEM((rows, 128), BF16),
            pltpu.VMEM((shards, PAD, 128), BF16),
            pltpu.VMEM((rows, 128), BF16),
            pltpu.VMEM((3, rows, rows), BF16),
            pltpu.SemaphoreType.DMA((3 + WIDE // 512 + CHUNKS,)),
            pltpu.SemaphoreType.DMA((3,)),
            pltpu.SemaphoreType.DMA((1,)),
            pltpu.SemaphoreType.DMA((3 * CHUNKS,)),
            pltpu.SemaphoreType.DMA((CHUNKS,)),
            pltpu.SemaphoreType.DMA((4 * CHUNKS,)),
            pltpu.SemaphoreType.DMA((4,)),
            pltpu.SemaphoreType.REGULAR((4,)),
        ],
        compiler_params=pltpu.CompilerParams(
            collective_id=0, has_side_effects=True, vmem_limit_bytes=60 << 20
        ),
        cost_estimate=pl.CostEstimate(
            flops=2 * rows * ff * width, bytes_accessed=2 * ff * (width + WIDE), transcendentals=0
        ),
    )(cotangent, hidden, down_weight, adapter_in, adapter_out, ids, segment_dirs)
    return pl.pallas_call(
        functools.partial(write_kernel, own),
        out_shape=(
            jax.ShapeDtypeStruct((tokens, ff), BF16),
            jax.ShapeDtypeStruct((ff, WIDE), F32),
            jax.ShapeDtypeStruct((WIDE, share), F32),
        ),
        in_specs=[any_space] * 5 + [vmem, smem],
        out_specs=(any_space,) * 3,
        scratch_shapes=[
            pltpu.VMEM((rows, 128), BF16),
            pltpu.VMEM((rows, share), BF16),
            pltpu.VMEM((tokens, ff), BF16),
            pltpu.VMEM((ff, rows), F32),
            pltpu.VMEM((ff, 128 * segment_dirs.shape[0]), BF16),
            pltpu.VMEM((tokens, ff), BF16),
            pltpu.VMEM((ff, WIDE), F32),
            pltpu.VMEM((WIDE, share), F32),
            pltpu.VMEM((tokens, WIDE), BF16),
            pltpu.VMEM((rows, WIDE), BF16),
            pltpu.SemaphoreType.DMA((4,)),
            pltpu.SemaphoreType.DMA((segment_dirs.shape[0],)),
            pltpu.SemaphoreType.DMA((1 + ff // 256 + WIDE // 512,)),
        ],
        compiler_params=pltpu.CompilerParams(vmem_limit_bytes=60 << 20),
        cost_estimate=pl.CostEstimate(
            flops=2 * tokens * ff * WIDE, bytes_accessed=4 * WIDE * (ff + share), transcendentals=0
        ),
    )(acc, low, cols, hidden, adapter_in, ids, segment_dirs)


def solution(mesh):
    def body(cotangent, hidden, *rest):
        own, width = cotangent.shape
        ff = hidden.shape[1]
        share = width // mesh.shape["tensor"]
        fits = (
            mesh.shape["tensor"] == 16
            and own == 12
            and hidden.shape[0] == 16 * own
            and width % (4 * CHUNKS * 128) == 0
            and share % 128 == 0
            and ff % 256 == 0
        )
        return (per_device if fits else per_device_plain)(cotangent, hidden, *rest)

    return jax.shard_map(
        body,
        mesh=mesh,
        in_specs=(
            P(("parts", "tensor"), None),
            P("parts", "tensor"),
            P("tensor", None),
            P("tensor", None),
            P(None, "tensor"),
            P("parts"),
            P("parts"),
        ),
        out_specs=(P("parts", "tensor"), P(("parts", "tensor"), None), P("parts", "tensor")),
        check_vma=False,
    )
```

```python
import functools

import jax
import jax.numpy as jnp
from jax import lax
from jax.experimental import pallas as pl
from jax.experimental.pallas import tpu as pltpu
from jax.sharding import PartitionSpec as P

RANK = 64
NUM_DIR = 40
WIDE = RANK * NUM_DIR
MESH = pl.DeviceIdType.MESH
F32 = jnp.float32
BF16 = jnp.bfloat16
NT = (((1,), (1,)), ((), ()))
TN = (((0,), (0,)), ((), ()))
NN = (((1,), (0,)), ((), ()))
PAD = 16
CHUNKS = 4


def dot(lhs, rhs, dims, **kw):
    return lax.dot_general(lhs, rhs, dims, preferred_element_type=F32, **kw)


def iota(shape, axis):
    return lax.broadcasted_iota(jnp.int32, shape, axis)


def direction_table(segment_ids, segment_dirs):
    seg_hot = (
        segment_ids[:, None] == jnp.arange(segment_dirs.shape[0], dtype=jnp.int32)[None, :]
    ).astype(F32)
    dir_hot = (segment_dirs[:, None] == jnp.arange(NUM_DIR, dtype=jnp.int32)[None, :]).astype(F32)
    return jnp.dot(seg_hot, dir_hot, precision=lax.Precision.HIGHEST)


def select_rank(wide, onehot):
    count = wide.shape[0]
    return jnp.sum(wide.reshape(count, NUM_DIR, RANK) * onehot[:, :, None], axis=1)


def spread_rank(low, onehot):
    count = low.shape[0]
    return (
        (0.5 * onehot[:, :, None] * low[:, None, :]).reshape(count, NUM_DIR * RANK).astype(BF16)
    )


def per_device_plain(
    cotangent, hidden, down_weight, adapter_in, adapter_out, segment_ids, segment_dirs
):
    onehot = direction_table(segment_ids, segment_dirs)
    width_share = adapter_out.shape[1]
    shards = cotangent.shape[1] // width_share
    own = cotangent.shape[0]
    full_rows = lax.all_gather(cotangent, "tensor", axis=0, tiled=True)
    pieces = cotangent.reshape(own, shards, width_share).transpose(1, 0, 2)
    columns = lax.all_to_all(pieces, "tensor", 0, 0, tiled=True).reshape(shards * own, width_share)
    wide_u = dot(columns, adapter_out, NT)
    wide_v = dot(hidden, adapter_in, NN)
    part = jnp.concatenate([select_rank(wide_u, onehot), select_rank(wide_v, onehot)], axis=1)
    low = lax.psum(part, "tensor")
    spread_u = spread_rank(low[:, :RANK], onehot)
    spread_v = spread_rank(low[:, RANK:], onehot)
    grad_in = dot(hidden, spread_u, TN)
    grad_out = dot(spread_v, columns, TN)
    base = dot(full_rows, down_weight, NT)
    extra = dot(spread_u, adapter_in, NT)
    return ((base + extra).astype(BF16), grad_in, grad_out)


def number_columns(place, number_row):
    ones = jnp.ones((place.shape[1], 128), BF16)
    return dot((place * (number_row + 1.0)).astype(BF16), ones, NN) - 1.0


def padded_place(own, tokens, rows, flip):
    shape = (tokens, rows) if flip else (rows, tokens)
    row, token = (iota(shape, 1), iota(shape, 0)) if flip else (iota(shape, 0), iota(shape, 1))
    inside = lax.rem(row, PAD)
    return ((token == own * (row // PAD) + inside) & (inside < own)).astype(F32)


def half_shift(shape):
    return (iota(shape, 1) >= RANK).astype(F32)


def main_kernel(
    cot_hbm, hid_hbm, dw_hbm, ain_hbm, aout_hbm, ids_ref, dirs_ref,
    acc_hbm, low_hbm, cols_hbm,
    cot, gat, fourth, dw, ain, aout, hid, acc, wide_cols, lpart, rpart, low, perm,
    ld_sem, st_sem, gs_sem, gr_sem, sib_sem, x_sem, cs_sem, chain_sem,
):
    own, width = cot_hbm.shape
    tokens, ff = hid_hbm.shape
    share = aout_hbm.shape[1]
    shards = width // share
    rows = shards * PAD
    quarter = width // 4
    step = quarter // CHUNKS

    p = lax.axis_index("parts")
    me = lax.axis_index("tensor")
    z, x, c = me // 4, lax.rem(me // 2, 2), lax.rem(me, 2)
    zs = [z, z + 1 - 2 * lax.rem(z, 2), lax.rem(z + 2, 4), 3 - z]

    def index(zz, xx, cc):
        return zz * 4 + xx * 2 + cc

    sib = index(z, x, 1 - c)
    xnb = index(z, 1 - x, c)
    z1, z2, z3 = (index(zs[k], x, c) for k in (1, 2, 3))

    def dev(i):
        return (p, i)

    bar = pltpu.get_barrier_semaphore()
    for nb in (sib, xnb, z1, z2, z3):
        pl.semaphore_signal(bar, inc=1, device_id=dev(nb), device_id_type=MESH)

    ld_cot = pltpu.make_async_copy(cot_hbm, cot, ld_sem.at[0])
    ld_hid = pltpu.make_async_copy(hid_hbm, hid, ld_sem.at[1])
    ld_cot.start()
    ld_hid.start()
    n_ain = WIDE // 512
    ld_ain = []
    for i in range(n_ain):
        cut = pl.ds(512 * i, 512)
        ld_ain.append(
            pltpu.make_async_copy(ain_hbm.at[:, cut], ain.at[:, cut], ld_sem.at[2 + i])
        )
        ld_ain[-1].start()
    ld_aout = pltpu.make_async_copy(aout_hbm, aout, ld_sem.at[2 + n_ain])
    ld_aout.start()
    for q in range(CHUNKS):
        for j in range(4):
            cut = pl.ds(quarter * j + step * q, step)
            pltpu.make_async_copy(
                dw_hbm.at[:, cut], dw.at[:, cut], ld_sem.at[3 + n_ain + q]
            ).start()

    def wait_dw(q):
        cut = pl.ds(quarter * q, quarter)
        pltpu.make_async_copy(dw_hbm.at[:, cut], dw.at[:, cut], ld_sem.at[3 + n_ain + q]).wait()

    def rows_of(b):
        return pl.ds(pl.multiple_of(b * PAD, PAD), PAD)

    def piece(b, q):
        return gat.at[:, rows_of(b), pl.ds(step * q, step)]

    def send(b, q, to, sem, recv):
        pltpu.make_async_remote_copy(
            src_ref=piece(b, q), dst_ref=piece(b, q), send_sem=sem, recv_sem=recv,
            device_id=dev(to), device_id_type=MESH,
        ).start()

    def arrived(b, q, sem):
        pltpu.make_async_copy(piece(b, q), piece(b, q), sem).wait()

    def col_block(k):
        return index(zs[k], x, c)

    def x_block(k):
        return index(zs[k], 1 - x, c)

    def send_own(q):
        send(me, q, xnb, gs_sem.at[0], x_sem.at[q])
        for k, to in ((1, z1), (2, z2), (3, z3)):
            send(me, q, to, gs_sem.at[0], gr_sem.at[(k - 1) * CHUNKS + q])
        send(me, q, sib, gs_sem.at[0], sib_sem.at[q])

    def take_column(k, q):
        b = col_block(k)
        arrived(b, q, gr_sem.at[(k - 1) * CHUNKS + q])
        send(b, q, xnb, gs_sem.at[0], x_sem.at[k * CHUNKS + q])
        send(b, q, sib, gs_sem.at[0], sib_sem.at[q])

    def take_x(k, q):
        b = x_block(k)
        arrived(b, q, x_sem.at[k * CHUNKS + q])
        send(b, q, sib, gs_sem.at[0], sib_sem.at[q])

    def take_sib(q):
        half = gat.at[:, pl.ds(0, rows // 2), pl.ds(step * q, step)]
        pltpu.make_async_copy(half, half, sib_sem.at[q]).wait()

    chain = (z1, z2, xnb, sib)

    def greet(i):
        pl.semaphore_signal(chain_sem.at[i], inc=1, device_id=dev(chain[i]), device_id_type=MESH)

    def greeted(i):
        pl.semaphore_wait(chain_sem.at[i], 1)

    ld_cot.wait()
    cot32 = cot[...].astype(F32)
    gap = PAD - own
    for j in range(3):
        tile = jnp.concatenate(
            [
                cot32[:, quarter * j : quarter * (j + 1)],
                cot32[gap * j : gap * (j + 1), 3 * quarter :],
            ],
            axis=0,
        )
        gat[j, rows_of(me), :] = tile.astype(BF16)
    pl.semaphore_wait(bar, 5)
    for q in range(CHUNKS):
        send_own(q)
    greet(0)

    dir_row = jnp.zeros((1, tokens), F32)
    ids = ids_ref[...]
    for s in range(dirs_ref.shape[0]):
        dir_row = jnp.where(ids == s, dirs_ref[s].astype(F32), dir_row)
    pad_place = padded_place(own, tokens, rows, False)
    dense_place = (iota((tokens, tokens), 0) == iota((tokens, tokens), 1)).astype(F32)
    dirs_dense = number_columns(dense_place, dir_row) - half_shift((tokens, 128))
    dirs_pad = number_columns(pad_place, dir_row) - half_shift((rows, 128))
    for j in range(3):
        a, b = iota((rows, rows), 0), iota((rows, rows), 1)
        ra, rb = lax.rem(a, PAD), lax.rem(b, PAD)
        hit = (a // PAD == b // PAD) & (ra // gap == j) & (rb - own == ra - gap * j)
        perm[j] = hit.astype(BF16)

    def pick(total, wide, where, first):
        for i in range(wide.shape[1] // 128):
            total = total + jnp.where(
                where == float(first + 2 * i), wide[:, 128 * i : 128 * (i + 1)], 0.0
            )
        return total

    ld_hid.wait()
    tot_v = jnp.zeros((tokens, 128), F32)
    for i in range(n_ain):
        ld_ain[i].wait()
        wide = dot(hid[...], ain[:, 512 * i : 512 * (i + 1)], NN)
        tot_v = pick(tot_v, wide, dirs_dense, 8 * i)
        if i == 1:
            greeted(0)
            greet(1)
            take_column(1, 0)
            take_column(2, 0)
    take_column(3, 0)
    take_column(1, 1)
    tot_v = dot(pad_place, tot_v, NN, precision=lax.Precision.HIGHEST)
    v = tot_v + pltpu.roll(tot_v, RANK, 1)

    greeted(1)
    greet(2)
    take_x(0, 0)
    take_x(1, 0)
    take_x(2, 0)
    take_x(3, 0)
    take_column(2, 1)
    take_column(3, 1)
    greeted(2)
    greet(3)
    ld_aout.wait()

    def assemble(q):
        cut = pl.ds(step * q, step)
        total = dot(perm[0], gat[0, :, cut], NN)
        total += dot(perm[1], gat[1, :, cut], NN)
        total += dot(perm[2], gat[2, :, cut], NN)
        fourth[:, cut] = total.astype(BF16)

    tile = ff // 2

    def base(q, h):
        r = pl.ds(tile * h, tile)
        total = acc[r, :] if q > 0 else None
        for j in range(4):
            cut = slice(quarter * j + step * q, quarter * j + step * (q + 1))
            rhs = (fourth if j == 3 else gat.at[j])[:, step * q : step * (q + 1)]
            add = dot(dw[r, cut], rhs, NT)
            total = add if total is None else total + add
        acc[r, :] = total

    def stage(q):
        take_sib(q)
        wait_dw(q)
        assemble(q)

    take_column(1, 2)
    take_column(2, 2)
    take_column(3, 2)
    take_x(0, 1)
    take_x(1, 1)
    take_x(2, 1)
    take_x(3, 1)
    take_column(1, 3)
    take_column(2, 3)
    take_column(3, 3)
    stage(0)
    greeted(3)
    take_x(0, 2)
    take_x(1, 2)
    take_x(2, 2)
    take_x(3, 2)
    take_x(0, 3)
    take_x(1, 3)
    stage(1)
    stage(2)
    take_x(2, 3)
    take_x(3, 3)
    stage(3)

    own_cols = pl.ds(pl.multiple_of((2 * x + c) * share, share), share)

    @pl.when(z < 3)
    def _():
        wide_cols[...] = gat[lax.rem(z, 3), :, own_cols]

    @pl.when(z == 3)
    def _():
        wide_cols[...] = fourth[:, own_cols]

    tot_u = jnp.zeros((rows, 128), F32)
    for i in range(n_ain):
        wide = dot(wide_cols[...], aout[512 * i : 512 * (i + 1), :], NT)
        tot_u = pick(tot_u, wide, dirs_pad, 8 * i)
    u = tot_u + pltpu.roll(tot_u, RANK, 1)
    lpart[...] = jnp.where(iota((rows, 128), 1) < RANK, u, v).astype(BF16)
    for i in range(1, shards):
        d = lax.rem(me + i, shards)
        pltpu.make_async_remote_copy(
            src_ref=lpart.at[rows_of(d), :], dst_ref=rpart.at[me],
            send_sem=cs_sem.at[0], recv_sem=cs_sem.at[1],
            device_id=dev(d), device_id_type=MESH,
        ).start()
    rpart[me] = lpart[rows_of(me), :]
    put_cols = pltpu.make_async_copy(wide_cols, cols_hbm, st_sem.at[0])
    put_cols.start()
    base(0, 0)
    base(0, 1)
    base(1, 0)
    base(1, 1)
    pieces = rpart.at[pl.ds(0, shards - 1)]
    pltpu.make_async_copy(pieces, pieces, cs_sem.at[1]).wait()
    summed = rpart[0].astype(F32)
    for i in range(1, shards):
        summed = summed + rpart[i].astype(F32)
    low[rows_of(me), :] = (0.5 * summed).astype(BF16)
    for i in range(1, shards):
        d = lax.rem(me + i, shards)
        pltpu.make_async_remote_copy(
            src_ref=low.at[rows_of(me), :], dst_ref=low.at[rows_of(me), :],
            send_sem=cs_sem.at[2], recv_sem=cs_sem.at[3],
            device_id=dev(d), device_id_type=MESH,
        ).start()
    base(2, 0)
    base(2, 1)
    base(3, 0)
    base(3, 1)
    put_acc = pltpu.make_async_copy(acc, acc_hbm, st_sem.at[2])
    put_acc.start()
    known = low.at[pl.ds(0, rows - PAD), :]
    pltpu.make_async_copy(known, known, cs_sem.at[3]).wait()
    put_low = pltpu.make_async_copy(low, low_hbm, st_sem.at[1])
    put_low.start()

    def left(units, sem):
        sent = gat.at[:, pl.ds(0, units * PAD), :]
        pltpu.make_async_copy(sent, sent, sem).wait()

    left(15, gs_sem.at[0])
    pltpu.make_async_copy(pieces, pieces, cs_sem.at[0]).wait()
    pltpu.make_async_copy(known, known, cs_sem.at[2]).wait()
    for put in (put_cols, put_acc, put_low):
        put.wait()


def write_kernel(
    own, acc_in, low_in, cols_in, hid_in, ain_in, ids_ref, dirs_ref,
    gh_hbm, gin_hbm, gout_hbm,
    low, cols, hid, acc, asel, gh, gin, gout, spread, spread_v, ld_sem, ain_sem, out_sem,
):
    tokens, ff = hid_in.shape
    rows = low_in.shape[0]
    segs = dirs_ref.shape[0]
    loads = [
        pltpu.make_async_copy(src, dst, ld_sem.at[i])
        for i, (src, dst) in enumerate(((low_in, low), (hid_in, hid), (cols_in, cols), (acc_in, acc)))
    ]
    for load in loads:
        load.start()
    for s in range(segs):
        start = pl.multiple_of((dirs_ref[s] // 2) * 128, 128)
        pltpu.make_async_copy(
            ain_in.at[:, pl.ds(start, 128)], asel.at[:, pl.ds(128 * s, 128)], ain_sem.at[s]
        ).start()
    dir_row = jnp.zeros((1, tokens), F32)
    ids = ids_ref[...]
    for s in range(segs):
        dir_row = jnp.where(ids == s, dirs_ref[s].astype(F32), dir_row)
    pad_place = padded_place(own, tokens, rows, False)
    dense_place = (iota((tokens, tokens), 0) == iota((tokens, tokens), 1)).astype(F32)
    dirs_dense = number_columns(dense_place, dir_row) - half_shift((tokens, 128))
    dirs_pad = number_columns(pad_place, dir_row) - half_shift((rows, 128))
    place = padded_place(own, tokens, rows, True).astype(BF16)
    loads[0].wait()
    dense = dot(place, low[...], NN)
    u_twice = jnp.where(iota((tokens, 128), 1) < RANK, dense, pltpu.roll(dense, RANK, 1))
    for i in range(NUM_DIR // 2):
        spread[:, 128 * i : 128 * (i + 1)] = jnp.where(
            dirs_dense == float(2 * i), u_twice, 0.0
        ).astype(BF16)
    loads[1].wait()
    puts = []

    def put(src, dst):
        puts.append(pltpu.make_async_copy(src, dst, out_sem.at[len(puts)]))
        puts[-1].start()

    tile = 256
    for i in range(ff // tile):
        r = pl.ds(tile * i, tile)
        gin[r, :] = dot(hid[:, tile * i : tile * (i + 1)], spread[...], TN)
        put(gin.at[r, :], gin_hbm.at[r, :])

    both = low[...].astype(F32)
    u_pad = jnp.where(iota((rows, 128), 1) < RANK, both, pltpu.roll(both, RANK, 1))
    v_pad = jnp.where(iota((rows, 128), 1) < RANK, pltpu.roll(both, RANK, 1), both)
    for i in range(NUM_DIR // 2):
        spread_v[:, 128 * i : 128 * (i + 1)] = jnp.where(
            dirs_pad == float(2 * i), v_pad, 0.0
        ).astype(BF16)
    loads[2].wait()
    for i in range(WIDE // 512):
        r = pl.ds(512 * i, 512)
        gout[r, :] = dot(spread_v[:, 512 * i : 512 * (i + 1)], cols[...], TN)
        put(gout.at[r, :], gout_hbm.at[r, :])

    code = 2.0 * number_columns(pad_place, ids.astype(F32)) + half_shift((rows, 128))
    spread_pad = jnp.concatenate(
        [
            jnp.where(code == (2 * s + lax.rem(dirs_ref[s], 2)).astype(F32), u_pad, 0.0).astype(BF16)
            for s in range(segs)
        ],
        axis=1,
    )
    for s in range(segs):
        pltpu.make_async_copy(
            ain_in.at[:, pl.ds(0, 128)], asel.at[:, pl.ds(128 * s, 128)], ain_sem.at[s]
        ).wait()
    loads[3].wait()
    for h in range(2):
        r = pl.ds(ff // 2 * h, ff // 2)
        total = acc[r, :] + dot(asel[r, :], spread_pad, NT)
        gh[:, r] = dot(place, total.astype(BF16), NT).astype(BF16)
    put(gh, gh_hbm)
    for copy in puts:
        copy.wait()


def per_device(cotangent, hidden, down_weight, adapter_in, adapter_out, segment_ids, segment_dirs):
    own, width = cotangent.shape
    tokens, ff = hidden.shape
    share = adapter_out.shape[1]
    shards = width // share
    rows = shards * PAD
    ids = segment_ids.reshape(1, tokens)
    any_space = pl.BlockSpec(memory_space=pl.ANY)
    vmem = pl.BlockSpec(memory_space=pltpu.VMEM)
    smem = pl.BlockSpec(memory_space=pltpu.SMEM)
    acc, low, cols = pl.pallas_call(
        main_kernel,
        out_shape=(
            jax.ShapeDtypeStruct((ff, rows), F32),
            jax.ShapeDtypeStruct((rows, 128), BF16),
            jax.ShapeDtypeStruct((rows, share), BF16),
        ),
        in_specs=[any_space] * 5 + [vmem, smem],
        out_specs=(any_space,) * 3,
        scratch_shapes=[
            pltpu.VMEM((own, width), BF16),
            pltpu.VMEM((3, rows, width // 4), BF16),
            pltpu.VMEM((rows, width // 4), BF16),
            pltpu.VMEM((ff, width), BF16),
            pltpu.VMEM((ff, WIDE), BF16),
            pltpu.VMEM((WIDE, share), BF16),
            pltpu.VMEM((tokens, ff), BF16),
            pltpu.VMEM((ff, rows), F32),
            pltpu.VMEM((rows, share), BF16),
            pltpu.VMEM((rows, 128), BF16),
            pltpu.VMEM((shards, PAD, 128), BF16),
            pltpu.VMEM((rows, 128), BF16),
            pltpu.VMEM((3, rows, rows), BF16),
            pltpu.SemaphoreType.DMA((3 + WIDE // 512 + CHUNKS,)),
            pltpu.SemaphoreType.DMA((3,)),
            pltpu.SemaphoreType.DMA((1,)),
            pltpu.SemaphoreType.DMA((3 * CHUNKS,)),
            pltpu.SemaphoreType.DMA((CHUNKS,)),
            pltpu.SemaphoreType.DMA((4 * CHUNKS,)),
            pltpu.SemaphoreType.DMA((4,)),
            pltpu.SemaphoreType.REGULAR((4,)),
        ],
        compiler_params=pltpu.CompilerParams(
            collective_id=0, has_side_effects=True, vmem_limit_bytes=60 << 20
        ),
        cost_estimate=pl.CostEstimate(
            flops=2 * rows * ff * width, bytes_accessed=2 * ff * (width + WIDE), transcendentals=0
        ),
    )(cotangent, hidden, down_weight, adapter_in, adapter_out, ids, segment_dirs)
    return pl.pallas_call(
        functools.partial(write_kernel, own),
        out_shape=(
            jax.ShapeDtypeStruct((tokens, ff), BF16),
            jax.ShapeDtypeStruct((ff, WIDE), F32),
            jax.ShapeDtypeStruct((WIDE, share), F32),
        ),
        in_specs=[any_space] * 5 + [vmem, smem],
        out_specs=(any_space,) * 3,
        scratch_shapes=[
            pltpu.VMEM((rows, 128), BF16),
            pltpu.VMEM((rows, share), BF16),
            pltpu.VMEM((tokens, ff), BF16),
            pltpu.VMEM((ff, rows), F32),
            pltpu.VMEM((ff, 128 * segment_dirs.shape[0]), BF16),
            pltpu.VMEM((tokens, ff), BF16),
            pltpu.VMEM((ff, WIDE), F32),
            pltpu.VMEM((WIDE, share), F32),
            pltpu.VMEM((tokens, WIDE), BF16),
            pltpu.VMEM((rows, WIDE), BF16),
            pltpu.SemaphoreType.DMA((4,)),
            pltpu.SemaphoreType.DMA((segment_dirs.shape[0],)),
            pltpu.SemaphoreType.DMA((1 + ff // 256 + WIDE // 512,)),
        ],
        compiler_params=pltpu.CompilerParams(vmem_limit_bytes=60 << 20),
        cost_estimate=pl.CostEstimate(
            flops=2 * tokens * ff * WIDE, bytes_accessed=4 * WIDE * (ff + share), transcendentals=0
        ),
    )(acc, low, cols, hidden, adapter_in, ids, segment_dirs)


def solution(mesh):
    def body(cotangent, hidden, *rest):
        own, width = cotangent.shape
        ff = hidden.shape[1]
        share = width // mesh.shape["tensor"]
        fits = (
            mesh.shape["tensor"] == 16
            and own == 12
            and hidden.shape[0] == 16 * own
            and width % (4 * CHUNKS * 128) == 0
            and share % 128 == 0
            and ff % 256 == 0
        )
        return (per_device if fits else per_device_plain)(cotangent, hidden, *rest)

    return jax.shard_map(
        body,
        mesh=mesh,
        in_specs=(
            P(("parts", "tensor"), None),
            P("parts", "tensor"),
            P("tensor", None),
            P("tensor", None),
            P(None, "tensor"),
            P("parts"),
            P("parts"),
        ),
        out_specs=(P("parts", "tensor"), P(("parts", "tensor"), None), P("parts", "tensor")),
        check_vma=False,
    )
```

```python
import functools

import jax
import jax.numpy as jnp
from jax import lax
from jax.experimental import pallas as pl
from jax.experimental.pallas import tpu as pltpu
from jax.sharding import PartitionSpec as P

RANK = 64
NUM_DIR = 40
WIDE = RANK * NUM_DIR
MESH = pl.DeviceIdType.MESH
F32 = jnp.float32
BF16 = jnp.bfloat16
NT = (((1,), (1,)), ((), ()))
TN = (((0,), (0,)), ((), ()))
NN = (((1,), (0,)), ((), ()))
PAD = 16
CHUNKS = 4


def dot(lhs, rhs, dims, **kw):
    return lax.dot_general(lhs, rhs, dims, preferred_element_type=F32, **kw)


def iota(shape, axis):
    return lax.broadcasted_iota(jnp.int32, shape, axis)


def direction_table(segment_ids, segment_dirs):
    seg_hot = (
        segment_ids[:, None] == jnp.arange(segment_dirs.shape[0], dtype=jnp.int32)[None, :]
    ).astype(F32)
    dir_hot = (segment_dirs[:, None] == jnp.arange(NUM_DIR, dtype=jnp.int32)[None, :]).astype(F32)
    return jnp.dot(seg_hot, dir_hot, precision=lax.Precision.HIGHEST)


def select_rank(wide, onehot):
    count = wide.shape[0]
    return jnp.sum(wide.reshape(count, NUM_DIR, RANK) * onehot[:, :, None], axis=1)


def spread_rank(low, onehot):
    count = low.shape[0]
    return (
        (0.5 * onehot[:, :, None] * low[:, None, :]).reshape(count, NUM_DIR * RANK).astype(BF16)
    )


def per_device_plain(
    cotangent, hidden, down_weight, adapter_in, adapter_out, segment_ids, segment_dirs
):
    onehot = direction_table(segment_ids, segment_dirs)
    width_share = adapter_out.shape[1]
    shards = cotangent.shape[1] // width_share
    own = cotangent.shape[0]
    full_rows = lax.all_gather(cotangent, "tensor", axis=0, tiled=True)
    pieces = cotangent.reshape(own, shards, width_share).transpose(1, 0, 2)
    columns = lax.all_to_all(pieces, "tensor", 0, 0, tiled=True).reshape(shards * own, width_share)
    wide_u = dot(columns, adapter_out, NT)
    wide_v = dot(hidden, adapter_in, NN)
    part = jnp.concatenate([select_rank(wide_u, onehot), select_rank(wide_v, onehot)], axis=1)
    low = lax.psum(part, "tensor")
    spread_u = spread_rank(low[:, :RANK], onehot)
    spread_v = spread_rank(low[:, RANK:], onehot)
    grad_in = dot(hidden, spread_u, TN)
    grad_out = dot(spread_v, columns, TN)
    base = dot(full_rows, down_weight, NT)
    extra = dot(spread_u, adapter_in, NT)
    return ((base + extra).astype(BF16), grad_in, grad_out)


def number_columns(place, number_row):
    ones = jnp.ones((place.shape[1], 128), BF16)
    return dot((place * (number_row + 1.0)).astype(BF16), ones, NN) - 1.0


def padded_place(own, tokens, rows, flip):
    shape = (tokens, rows) if flip else (rows, tokens)
    row, token = (iota(shape, 1), iota(shape, 0)) if flip else (iota(shape, 0), iota(shape, 1))
    inside = lax.rem(row, PAD)
    return ((token == own * (row // PAD) + inside) & (inside < own)).astype(F32)


def half_shift(shape):
    return (iota(shape, 1) >= RANK).astype(F32)


def main_kernel(
    cot_hbm, hid_hbm, dw_hbm, ain_hbm, aout_hbm, ids_ref, dirs_ref,
    acc_hbm, low_hbm, cols_hbm,
    cot, gat, fourth, dw, ain, aout, hid, acc, wide_cols, lpart, rpart, low, perm,
    ld_sem, st_sem, gs_sem, gr_sem, sib_sem, x_sem, cs_sem, chain_sem,
):
    own, width = cot_hbm.shape
    tokens, ff = hid_hbm.shape
    share = aout_hbm.shape[1]
    shards = width // share
    rows = shards * PAD
    quarter = width // 4
    step = quarter // CHUNKS

    p = lax.axis_index("parts")
    me = lax.axis_index("tensor")
    z, x, c = me // 4, lax.rem(me // 2, 2), lax.rem(me, 2)
    zs = [z, z + 1 - 2 * lax.rem(z, 2), lax.rem(z + 2, 4), 3 - z]

    def index(zz, xx, cc):
        return zz * 4 + xx * 2 + cc

    sib = index(z, x, 1 - c)
    xnb = index(z, 1 - x, c)
    z1, z2, z3 = (index(zs[k], x, c) for k in (1, 2, 3))

    def dev(i):
        return (p, i)

    bar = pltpu.get_barrier_semaphore()
    for nb in (sib, xnb, z1, z2, z3):
        pl.semaphore_signal(bar, inc=1, device_id=dev(nb), device_id_type=MESH)

    ld_cot = pltpu.make_async_copy(cot_hbm, cot, ld_sem.at[0])
    ld_hid = pltpu.make_async_copy(hid_hbm, hid, ld_sem.at[1])
    ld_cot.start()
    ld_hid.start()
    n_ain = WIDE // 512
    ld_ain = []
    for i in range(n_ain):
        cut = pl.ds(512 * i, 512)
        ld_ain.append(
            pltpu.make_async_copy(ain_hbm.at[:, cut], ain.at[:, cut], ld_sem.at[2 + i])
        )
        ld_ain[-1].start()
    ld_aout = pltpu.make_async_copy(aout_hbm, aout, ld_sem.at[2 + n_ain])
    ld_aout.start()
    for q in range(CHUNKS):
        for j in range(4):
            cut = pl.ds(quarter * j + step * q, step)
            pltpu.make_async_copy(
                dw_hbm.at[:, cut], dw.at[:, cut], ld_sem.at[3 + n_ain + q]
            ).start()

    def wait_dw(q):
        cut = pl.ds(quarter * q, quarter)
        pltpu.make_async_copy(dw_hbm.at[:, cut], dw.at[:, cut], ld_sem.at[3 + n_ain + q]).wait()

    def rows_of(b):
        return pl.ds(pl.multiple_of(b * PAD, PAD), PAD)

    def piece(b, q):
        return gat.at[:, rows_of(b), pl.ds(step * q, step)]

    def send(b, q, to, sem, recv):
        pltpu.make_async_remote_copy(
            src_ref=piece(b, q), dst_ref=piece(b, q), send_sem=sem, recv_sem=recv,
            device_id=dev(to), device_id_type=MESH,
        ).start()

    def arrived(b, q, sem):
        pltpu.make_async_copy(piece(b, q), piece(b, q), sem).wait()

    def col_block(k):
        return index(zs[k], x, c)

    def x_block(k):
        return index(zs[k], 1 - x, c)

    def send_own(q):
        send(me, q, xnb, gs_sem.at[0], x_sem.at[q])
        for k, to in ((1, z1), (2, z2), (3, z3)):
            send(me, q, to, gs_sem.at[0], gr_sem.at[(k - 1) * CHUNKS + q])
        send(me, q, sib, gs_sem.at[0], sib_sem.at[q])

    def take_column(k, q):
        b = col_block(k)
        arrived(b, q, gr_sem.at[(k - 1) * CHUNKS + q])
        send(b, q, xnb, gs_sem.at[0], x_sem.at[k * CHUNKS + q])
        send(b, q, sib, gs_sem.at[0], sib_sem.at[q])

    def take_x(k, q):
        b = x_block(k)
        arrived(b, q, x_sem.at[k * CHUNKS + q])
        send(b, q, sib, gs_sem.at[0], sib_sem.at[q])

    def take_sib(q):
        half = gat.at[:, pl.ds(0, rows // 2), pl.ds(step * q, step)]
        pltpu.make_async_copy(half, half, sib_sem.at[q]).wait()

    chain = (z1, z2, xnb, sib)

    def greet(i):
        pl.semaphore_signal(chain_sem.at[i], inc=1, device_id=dev(chain[i]), device_id_type=MESH)

    def greeted(i):
        pl.semaphore_wait(chain_sem.at[i], 1)

    ld_cot.wait()
    cot32 = cot[...].astype(F32)
    gap = PAD - own
    for j in range(3):
        tile = jnp.concatenate(
            [
                cot32[:, quarter * j : quarter * (j + 1)],
                cot32[gap * j : gap * (j + 1), 3 * quarter :],
            ],
            axis=0,
        )
        gat[j, rows_of(me), :] = tile.astype(BF16)
    pl.semaphore_wait(bar, 5)
    for q in range(CHUNKS):
        send_own(q)
    greet(0)

    dir_row = jnp.zeros((1, tokens), F32)
    ids = ids_ref[...]
    for s in range(dirs_ref.shape[0]):
        dir_row = jnp.where(ids == s, dirs_ref[s].astype(F32), dir_row)
    pad_place = padded_place(own, tokens, rows, False)
    dense_place = (iota((tokens, tokens), 0) == iota((tokens, tokens), 1)).astype(F32)
    dirs_dense = number_columns(dense_place, dir_row) - half_shift((tokens, 128))
    dirs_pad = number_columns(pad_place, dir_row) - half_shift((rows, 128))
    for j in range(3):
        a, b = iota((rows, rows), 0), iota((rows, rows), 1)
        ra, rb = lax.rem(a, PAD), lax.rem(b, PAD)
        hit = (a // PAD == b // PAD) & (ra // gap == j) & (rb - own == ra - gap * j)
        perm[j] = hit.astype(BF16)

    def pick(total, wide, where, first):
        for i in range(wide.shape[1] // 128):
            total = total + jnp.where(
                where == float(first + 2 * i), wide[:, 128 * i : 128 * (i + 1)], 0.0
            )
        return total

    ld_hid.wait()
    tot_v = jnp.zeros((tokens, 128), F32)
    for i in range(n_ain):
        ld_ain[i].wait()
        wide = dot(hid[...], ain[:, 512 * i : 512 * (i + 1)], NN)
        tot_v = pick(tot_v, wide, dirs_dense, 8 * i)
        if i == 1:
            greeted(0)
            greet(1)
            take_column(1, 0)
            take_column(2, 0)
    take_column(3, 0)
    take_column(1, 1)
    tot_v = dot(pad_place, tot_v, NN, precision=lax.Precision.HIGHEST)
    v = tot_v + pltpu.roll(tot_v, RANK, 1)

    greeted(1)
    greet(2)
    take_x(0, 0)
    take_x(1, 0)
    take_x(2, 0)
    take_x(3, 0)
    take_column(2, 1)
    take_column(3, 1)
    greeted(2)
    greet(3)
    ld_aout.wait()

    def assemble(q):
        cut = pl.ds(step * q, step)
        total = dot(perm[0], gat[0, :, cut], NN)
        total += dot(perm[1], gat[1, :, cut], NN)
        total += dot(perm[2], gat[2, :, cut], NN)
        fourth[:, cut] = total.astype(BF16)

    tile = ff // 2

    def base(q, h):
        r = pl.ds(tile * h, tile)
        total = acc[r, :] if q > 0 else None
        for j in range(4):
            cut = slice(quarter * j + step * q, quarter * j + step * (q + 1))
            rhs = (fourth if j == 3 else gat.at[j])[:, step * q : step * (q + 1)]
            add = dot(dw[r, cut], rhs, NT)
            total = add if total is None else total + add
        acc[r, :] = total

    def stage(q):
        take_sib(q)
        wait_dw(q)
        assemble(q)

    take_column(1, 2)
    take_column(2, 2)
    take_column(3, 2)
    take_x(0, 1)
    take_x(1, 1)
    take_x(2, 1)
    take_x(3, 1)
    take_column(1, 3)
    take_column(2, 3)
    take_column(3, 3)
    stage(0)
    greeted(3)
    take_x(0, 2)
    take_x(1, 2)
    take_x(2, 2)
    take_x(3, 2)
    take_x(0, 3)
    take_x(1, 3)
    stage(1)
    stage(2)
    take_x(2, 3)
    take_x(3, 3)
    stage(3)

    own_cols = pl.ds(pl.multiple_of((2 * x + c) * share, share), share)

    @pl.when(z < 3)
    def _():
        wide_cols[...] = gat[lax.rem(z, 3), :, own_cols]

    @pl.when(z == 3)
    def _():
        wide_cols[...] = fourth[:, own_cols]

    tot_u = jnp.zeros((rows, 128), F32)
    for i in range(n_ain):
        wide = dot(wide_cols[...], aout[512 * i : 512 * (i + 1), :], NT)
        tot_u = pick(tot_u, wide, dirs_pad, 8 * i)
    u = tot_u + pltpu.roll(tot_u, RANK, 1)
    lpart[...] = jnp.where(iota((rows, 128), 1) < RANK, u, v).astype(BF16)
    for i in range(1, shards):
        d = lax.rem(me + i, shards)
        pltpu.make_async_remote_copy(
            src_ref=lpart.at[rows_of(d), :], dst_ref=rpart.at[me],
            send_sem=cs_sem.at[0], recv_sem=cs_sem.at[1],
            device_id=dev(d), device_id_type=MESH,
        ).start()
    rpart[me] = lpart[rows_of(me), :]
    put_cols = pltpu.make_async_copy(wide_cols, cols_hbm, st_sem.at[0])
    put_cols.start()
    base(0, 0)
    base(0, 1)
    base(1, 0)
    base(1, 1)
    pieces = rpart.at[pl.ds(0, shards - 1)]
    pltpu.make_async_copy(pieces, pieces, cs_sem.at[1]).wait()
    summed = rpart[0].astype(F32)
    for i in range(1, shards):
        summed = summed + rpart[i].astype(F32)
    low[rows_of(me), :] = (0.5 * summed).astype(BF16)
    for i in range(1, shards):
        d = lax.rem(me + i, shards)
        pltpu.make_async_remote_copy(
            src_ref=low.at[rows_of(me), :], dst_ref=low.at[rows_of(me), :],
            send_sem=cs_sem.at[2], recv_sem=cs_sem.at[3],
            device_id=dev(d), device_id_type=MESH,
        ).start()
    base(2, 0)
    base(2, 1)
    put_acc = []
    for h in range(2):
        base(3, h)
        r = pl.ds(tile * h, tile)
        put_acc.append(pltpu.make_async_copy(acc.at[r, :], acc_hbm.at[r, :], st_sem.at[2 + h]))
        put_acc[h].start()
    known = low.at[pl.ds(0, rows - PAD), :]
    pltpu.make_async_copy(known, known, cs_sem.at[3]).wait()
    put_low = pltpu.make_async_copy(low, low_hbm, st_sem.at[1])
    put_low.start()

    def left(units, sem):
        sent = gat.at[:, pl.ds(0, units * PAD), :]
        pltpu.make_async_copy(sent, sent, sem).wait()

    left(15, gs_sem.at[0])
    pltpu.make_async_copy(pieces, pieces, cs_sem.at[0]).wait()
    pltpu.make_async_copy(known, known, cs_sem.at[2]).wait()
    for put in (put_cols, put_low, *put_acc):
        put.wait()


def write_kernel(
    own, acc_in, low_in, cols_in, hid_in, ain_in, ids_ref, dirs_ref,
    gh_hbm, gin_hbm, gout_hbm,
    low, cols, hid, acc, asel, gh, gin, gout, spread, spread_v, ld_sem, ain_sem, out_sem,
):
    tokens, ff = hid_in.shape
    rows = low_in.shape[0]
    segs = dirs_ref.shape[0]
    loads = [
        pltpu.make_async_copy(src, dst, ld_sem.at[i])
        for i, (src, dst) in enumerate(((low_in, low), (hid_in, hid), (cols_in, cols), (acc_in, acc)))
    ]
    for load in loads:
        load.start()
    for s in range(segs):
        start = pl.multiple_of((dirs_ref[s] // 2) * 128, 128)
        pltpu.make_async_copy(
            ain_in.at[:, pl.ds(start, 128)], asel.at[:, pl.ds(128 * s, 128)], ain_sem.at[s]
        ).start()
    dir_row = jnp.zeros((1, tokens), F32)
    ids = ids_ref[...]
    for s in range(segs):
        dir_row = jnp.where(ids == s, dirs_ref[s].astype(F32), dir_row)
    pad_place = padded_place(own, tokens, rows, False)
    dense_place = (iota((tokens, tokens), 0) == iota((tokens, tokens), 1)).astype(F32)
    dirs_dense = number_columns(dense_place, dir_row) - half_shift((tokens, 128))
    dirs_pad = number_columns(pad_place, dir_row) - half_shift((rows, 128))
    place = padded_place(own, tokens, rows, True).astype(BF16)
    loads[0].wait()
    dense = dot(place, low[...], NN)
    u_twice = jnp.where(iota((tokens, 128), 1) < RANK, dense, pltpu.roll(dense, RANK, 1))
    for i in range(NUM_DIR // 2):
        spread[:, 128 * i : 128 * (i + 1)] = jnp.where(
            dirs_dense == float(2 * i), u_twice, 0.0
        ).astype(BF16)
    loads[1].wait()
    puts = []

    def put(src, dst):
        puts.append(pltpu.make_async_copy(src, dst, out_sem.at[len(puts)]))
        puts[-1].start()

    tile = 256
    for i in range(ff // tile):
        r = pl.ds(tile * i, tile)
        gin[r, :] = dot(hid[:, tile * i : tile * (i + 1)], spread[...], TN)
        put(gin.at[r, :], gin_hbm.at[r, :])

    both = low[...].astype(F32)
    u_pad = jnp.where(iota((rows, 128), 1) < RANK, both, pltpu.roll(both, RANK, 1))
    v_pad = jnp.where(iota((rows, 128), 1) < RANK, pltpu.roll(both, RANK, 1), both)
    for i in range(NUM_DIR // 2):
        spread_v[:, 128 * i : 128 * (i + 1)] = jnp.where(
            dirs_pad == float(2 * i), v_pad, 0.0
        ).astype(BF16)
    loads[2].wait()
    for i in range(WIDE // 512):
        r = pl.ds(512 * i, 512)
        gout[r, :] = dot(spread_v[:, 512 * i : 512 * (i + 1)], cols[...], TN)
        put(gout.at[r, :], gout_hbm.at[r, :])

    code = 2.0 * number_columns(pad_place, ids.astype(F32)) + half_shift((rows, 128))
    spread_pad = jnp.concatenate(
        [
            jnp.where(code == (2 * s + lax.rem(dirs_ref[s], 2)).astype(F32), u_pad, 0.0).astype(BF16)
            for s in range(segs)
        ],
        axis=1,
    )
    for s in range(segs):
        pltpu.make_async_copy(
            ain_in.at[:, pl.ds(0, 128)], asel.at[:, pl.ds(128 * s, 128)], ain_sem.at[s]
        ).wait()
    loads[3].wait()
    for h in range(2):
        r = pl.ds(ff // 2 * h, ff // 2)
        total = acc[r, :] + dot(asel[r, :], spread_pad, NT)
        gh[:, r] = dot(place, total.astype(BF16), NT).astype(BF16)
    put(gh, gh_hbm)
    for copy in puts:
        copy.wait()


def per_device(cotangent, hidden, down_weight, adapter_in, adapter_out, segment_ids, segment_dirs):
    own, width = cotangent.shape
    tokens, ff = hidden.shape
    share = adapter_out.shape[1]
    shards = width // share
    rows = shards * PAD
    ids = segment_ids.reshape(1, tokens)
    any_space = pl.BlockSpec(memory_space=pl.ANY)
    vmem = pl.BlockSpec(memory_space=pltpu.VMEM)
    smem = pl.BlockSpec(memory_space=pltpu.SMEM)
    acc, low, cols = pl.pallas_call(
        main_kernel,
        out_shape=(
            jax.ShapeDtypeStruct((ff, rows), F32),
            jax.ShapeDtypeStruct((rows, 128), BF16),
            jax.ShapeDtypeStruct((rows, share), BF16),
        ),
        in_specs=[any_space] * 5 + [vmem, smem],
        out_specs=(any_space,) * 3,
        scratch_shapes=[
            pltpu.VMEM((own, width), BF16),
            pltpu.VMEM((3, rows, width // 4), BF16),
            pltpu.VMEM((rows, width // 4), BF16),
            pltpu.VMEM((ff, width), BF16),
            pltpu.VMEM((ff, WIDE), BF16),
            pltpu.VMEM((WIDE, share), BF16),
            pltpu.VMEM((tokens, ff), BF16),
            pltpu.VMEM((ff, rows), F32),
            pltpu.VMEM((rows, share), BF16),
            pltpu.VMEM((rows, 128), BF16),
            pltpu.VMEM((shards, PAD, 128), BF16),
            pltpu.VMEM((rows, 128), BF16),
            pltpu.VMEM((3, rows, rows), BF16),
            pltpu.SemaphoreType.DMA((3 + WIDE // 512 + CHUNKS,)),
            pltpu.SemaphoreType.DMA((4,)),
            pltpu.SemaphoreType.DMA((1,)),
            pltpu.SemaphoreType.DMA((3 * CHUNKS,)),
            pltpu.SemaphoreType.DMA((CHUNKS,)),
            pltpu.SemaphoreType.DMA((4 * CHUNKS,)),
            pltpu.SemaphoreType.DMA((4,)),
            pltpu.SemaphoreType.REGULAR((4,)),
        ],
        compiler_params=pltpu.CompilerParams(
            collective_id=0, has_side_effects=True, vmem_limit_bytes=60 << 20
        ),
        cost_estimate=pl.CostEstimate(
            flops=2 * rows * ff * width, bytes_accessed=2 * ff * (width + WIDE), transcendentals=0
        ),
    )(cotangent, hidden, down_weight, adapter_in, adapter_out, ids, segment_dirs)
    return pl.pallas_call(
        functools.partial(write_kernel, own),
        out_shape=(
            jax.ShapeDtypeStruct((tokens, ff), BF16),
            jax.ShapeDtypeStruct((ff, WIDE), F32),
            jax.ShapeDtypeStruct((WIDE, share), F32),
        ),
        in_specs=[any_space] * 5 + [vmem, smem],
        out_specs=(any_space,) * 3,
        scratch_shapes=[
            pltpu.VMEM((rows, 128), BF16),
            pltpu.VMEM((rows, share), BF16),
            pltpu.VMEM((tokens, ff), BF16),
            pltpu.VMEM((ff, rows), F32),
            pltpu.VMEM((ff, 128 * segment_dirs.shape[0]), BF16),
            pltpu.VMEM((tokens, ff), BF16),
            pltpu.VMEM((ff, WIDE), F32),
            pltpu.VMEM((WIDE, share), F32),
            pltpu.VMEM((tokens, WIDE), BF16),
            pltpu.VMEM((rows, WIDE), BF16),
            pltpu.SemaphoreType.DMA((4,)),
            pltpu.SemaphoreType.DMA((segment_dirs.shape[0],)),
            pltpu.SemaphoreType.DMA((1 + ff // 256 + WIDE // 512,)),
        ],
        compiler_params=pltpu.CompilerParams(vmem_limit_bytes=60 << 20),
        cost_estimate=pl.CostEstimate(
            flops=2 * tokens * ff * WIDE, bytes_accessed=4 * WIDE * (ff + share), transcendentals=0
        ),
    )(acc, low, cols, hidden, adapter_in, ids, segment_dirs)


def solution(mesh):
    def body(cotangent, hidden, *rest):
        own, width = cotangent.shape
        ff = hidden.shape[1]
        share = width // mesh.shape["tensor"]
        fits = (
            mesh.shape["tensor"] == 16
            and own == 12
            and hidden.shape[0] == 16 * own
            and width % (4 * CHUNKS * 128) == 0
            and share % 128 == 0
            and ff % 256 == 0
        )
        return (per_device if fits else per_device_plain)(cotangent, hidden, *rest)

    return jax.shard_map(
        body,
        mesh=mesh,
        in_specs=(
            P(("parts", "tensor"), None),
            P("parts", "tensor"),
            P("tensor", None),
            P("tensor", None),
            P(None, "tensor"),
            P("parts"),
            P("parts"),
        ),
        out_specs=(P("parts", "tensor"), P(("parts", "tensor"), None), P("parts", "tensor")),
        check_vma=False,
    )
```
